128 devices in a mesh: dom: 32 (over z, x, core), dp: 4 (over y).
Axes of the slice: x: 4, y: 4, z: 4, core: 2. Of those that a mesh axis runs over, the one named last changes fastest.
Arguments:
- node_latents: bfloat16 [131072, 128], P(('dom', 'dp')), may hold values from -6 to 6
- mesh_latents: bfloat16 [393216, 128], P(('dom', 'dp')), may hold values from -6 to 6
- world_latents: bfloat16 [65536, 128], P(('dom', 'dp')), may hold values from -6 to 6
- mesh_src: int32 [393216], P(('dom', 'dp')), may hold values from 0 to 1535, as said below
- mesh_dst: int32 [393216], P(('dom', 'dp')), may hold values from 0 to 1023
- world_src: int32 [65536], P(('dom', 'dp')), may hold values from 0 to 8191, as said below
- world_dst: int32 [65536], P(('dom', 'dp')), may hold values from 0 to 1023
- send_blocks: int32 [128, 32, 16], P(('dom', 'dp')), may hold values from 0 to 63
- world_count: int32 [128], P(('dom', 'dp')), may hold values from 256 to 512, as said below
- node_cot: bfloat16 [131072, 128], P(('dom', 'dp')), may hold values from -6 to 6
- mesh_cot: bfloat16 [393216, 128], P(('dom', 'dp')), may hold values from -6 to 6
- world_cot: bfloat16 [65536, 128], P(('dom', 'dp')), may hold values from -6 to 6
- first_weights: bfloat16 [3, 384, 128], replicated, may hold values from -0.3125 to 0.3125
- rest_weights: bfloat16 [3, 2, 128, 128], replicated, may hold values from -0.5 to 0.5
- biases: float32 [3, 4, 128], replicated, may hold values from -2 to 2
- gains: float32 [3, 128], replicated, may hold values from 0.1 to 1.9
Outputs:
- new_nodes: bfloat16 [131072, 128], P(('dom', 'dp'))
- new_mesh: bfloat16 [393216, 128], P(('dom', 'dp'))
- new_world: bfloat16 [65536, 128], P(('dom', 'dp'))
- grad_nodes: bfloat16 [131072, 128], P(('dom', 'dp'))
- grad_mesh: bfloat16 [393216, 128], P(('dom', 'dp'))
- grad_world: bfloat16 [65536, 128], P(('dom', 'dp'))
- grad_first: float32 [3, 384, 128], replicated
- grad_rest: float32 [3, 2, 128, 128], replicated
- grad_biases: float32 [3, 4, 128], replicated
- grad_gains: float32 [3, 128], replicated
The draws below stay inside these ranges and needn't reach their ends.
Inputs may be any that keep to these rules, and one draw needn't show every extreme that they name: `mesh_src`: indexes the 256 rows before a partition's nodes (the last rows of the previous domain of its mesh), its 1024 nodes, then the 256 rows after (the first rows of the next domain); the first domain reads no rows before and the last none after. `world_src`: row j of slot t of the blocks sent by domain p of the same mesh is (p * 16 + t) * 16 + j; a partition reads some slots of each domain, all 16 for at least one. send_blocks[k, p, t] is the block of 16 node rows of partition k put in slot t for domain p of its mesh. Rows of partition k at or past world_count[k] are padding; some partition has all 512 rows live.
All inputs are finite; a program needn't handle non-finite values.
Results may differ from the reference program's by a relative error of at most 0.007.
Values may be sent and summed in bfloat16 or wider, within the bound.
A program may use at most 128 MiB of HBM per device.

```python
import jax
import jax.numpy as jnp
from jax import lax

D = 128
NODE_DEV = 1024
HALO = 256
BLK = 16
SLOTS = 16
MEDGE_DEV = 3072
WEDGE_DEV = 512
NODES = 131072
MEDGES = 393216
WEDGES = 65536
N_DOM = 32
N_DP = 4


def draw_mesh_src(key, part):
    key = jax.random.fold_in(key, 11)
    key_pick, key_left, key_right, key_inner = jax.random.split(key, 4)
    total_rows = MEDGE_DEV * N_DOM * N_DP
    device = jnp.arange(total_rows, dtype=jnp.int32) // MEDGE_DEV
    domain = device // N_DP
    picked = jax.random.randint(key_pick, (total_rows,), 0, 8)
    left_rows = jax.random.randint(key_left, (total_rows,), 0, HALO)
    right_rows = HALO + NODE_DEV + jax.random.randint(key_right, (total_rows,), 0, HALO)
    inner_rows = HALO + jax.random.randint(key_inner, (total_rows,), 0, NODE_DEV)
    chosen = jnp.where((picked == 0) & (domain > 0), left_rows, jnp.where((picked == 1) & (domain < N_DOM - 1), right_rows, inner_rows))
    return chosen.astype(jnp.int32)


def draw_world_src(key, part):
    key = jax.random.fold_in(key, 37)
    key_live, key_full, key_peer, key_slot, key_row = jax.random.split(key, 5)
    device_count = N_DOM * N_DP
    total_rows = WEDGE_DEV * device_count
    device = jnp.arange(total_rows, dtype=jnp.int32) // WEDGE_DEV
    live_slots = jax.random.randint(key_live, (device_count, N_DOM), 1, SLOTS + 1)
    full_peer = jax.random.randint(key_full, (device_count,), 0, N_DOM)
    live_slots = jnp.where(jnp.arange(N_DOM, dtype=jnp.int32)[None, :] == full_peer[:, None], SLOTS, live_slots)
    peer = jax.random.randint(key_peer, (total_rows,), 0, N_DOM)
    slot = jax.random.randint(key_slot, (total_rows,), 0, 65520) % live_slots[device, peer]
    row_within = jax.random.randint(key_row, (total_rows,), 0, BLK)
    return ((peer * SLOTS + slot) * BLK + row_within).astype(jnp.int32)


def draw_world_count(key, part):
    key = jax.random.fold_in(key, 23)
    key_one, key_top = jax.random.split(key, 2)
    device_count = N_DOM * N_DP
    counted = jax.random.randint(key_one, (device_count,), WEDGE_DEV // 2, WEDGE_DEV + 1)
    busiest = jax.random.randint(key_top, (), 0, device_count)
    counted = jnp.where(jnp.arange(device_count, dtype=jnp.int32) == busiest, WEDGE_DEV, counted)
    return counted.astype(jnp.int32)


def touch_ends(entries, key, low, largest):
    extent = entries.shape
    spot = [jax.random.randint(jax.random.fold_in(key, axis), (), 0, extent[axis]) for axis in range(len(extent))]
    entries = entries.at[tuple(spot)].set(low)
    longest = extent.index(max(extent))
    spot[longest] = (spot[longest] + 1) % extent[longest]
    return entries.at[tuple(spot)].set(largest)


def level_of(own_key, dims, pieces, low, top_value):
    gain, own = 1.0, jax.random.fold_in(own_key, 6)
    for axis_at, shards_of in pieces:
        heights = jnp.exp(jax.random.uniform(jax.random.fold_in(own, axis_at), (shards_of,), jnp.float32, low / len(pieces), top_value / len(pieces)))
        gain = gain * jnp.repeat(heights, dims[axis_at] // shards_of).reshape([-1 if axis == axis_at else 1 for axis in range(len(dims))])
    return gain


def normal_values(rng, shape, width, most, shards=(), kind=jnp.bfloat16):
    entries = jax.random.normal(rng, shape, jnp.float32) * width
    if len(shards) > 0:
        entries = level_of(rng, shape, shards, -0.22, 0.18) * entries
    return jnp.clip(entries, min=-most, max=most).astype(kind)


def setup_inputs(seed: int = 0) -> dict:
    seeds = jax.random.split(jax.random.key(seed), 17)
    node_latents = normal_values(seeds[0], (NODES, D), 1.0, 6.0, ((0, 128),))
    mesh_latents = normal_values(seeds[1], (MEDGES, D), 1.0, 6.0, ((0, 128),))
    world_latents = normal_values(seeds[2], (WEDGES, D), 1.0, 6.0, ((0, 128),))
    mesh_src = draw_mesh_src(jax.random.fold_in(seeds[16], 71), 0)
    mesh_dst = touch_ends(jax.random.randint(seeds[4], (MEDGES,), 0, NODE_DEV), jax.random.fold_in(seeds[4], 1), 0, NODE_DEV - 1).astype(jnp.int32)
    world_src = draw_world_src(jax.random.fold_in(seeds[16], 71), 0)
    world_dst = touch_ends(jax.random.randint(seeds[6], (WEDGES,), 0, NODE_DEV), jax.random.fold_in(seeds[6], 1), 0, NODE_DEV - 1).astype(jnp.int32)
    send_blocks = touch_ends(jax.random.randint(seeds[7], (N_DOM * N_DP, N_DOM, SLOTS), 0, NODE_DEV // BLK), jax.random.fold_in(seeds[7], 1), 0, (NODE_DEV // BLK) - 1).astype(jnp.int32)
    world_count = draw_world_count(jax.random.fold_in(seeds[16], 71), 0)
    node_cot = normal_values(seeds[9], (NODES, D), 1.0, 6.0, ((0, 128),))
    mesh_cot = normal_values(seeds[10], (MEDGES, D), 1.0, 6.0, ((0, 128),))
    world_cot = normal_values(seeds[11], (WEDGES, D), 1.0, 6.0, ((0, 128),))
    first_weights = normal_values(seeds[12], (3, 3 * D, D), (3 * D) ** -0.5, 0.3125)
    rest_weights = normal_values(seeds[13], (3, 2, D, D), D ** -0.5, 0.5)
    biases = normal_values(seeds[14], (3, 4, D), 0.3, 2.0, (), jnp.float32)
    gains = jnp.clip(1.0 + 0.18 * jax.random.normal(seeds[15], (3, D), jnp.float32), 0.1, 1.9)
    return dict(node_latents=node_latents, mesh_latents=mesh_latents, world_latents=world_latents, mesh_src=mesh_src, mesh_dst=mesh_dst, world_src=world_src, world_dst=world_dst, send_blocks=send_blocks, world_count=world_count, node_cot=node_cot, mesh_cot=mesh_cot, world_cot=world_cot, first_weights=first_weights, rest_weights=rest_weights, biases=biases, gains=gains)


norm_eps = 1e-05

def matmul(left, right):
    return jnp.dot(left, right, preferred_element_type=jnp.float32)

def matmul_nt(left, right):
    return lax.dot_general(left, right, (((1,), (1,)), ((), ())), preferred_element_type=jnp.float32)

def matmul_tn(left, right):
    return lax.dot_general(left, right, (((0,), (0,)), ((), ())), preferred_element_type=jnp.float32)

def silu_grad(values):
    sigma = jax.nn.sigmoid(values)
    return sigma * (1.0 + values * (1.0 - sigma))

def mlp_parts(inputs, first_w, rest_w, bias_rows, gain_row):
    pre_one = matmul(inputs, first_w) + bias_rows[0]
    act_one = jax.nn.silu(pre_one).astype(jnp.bfloat16)
    pre_two = matmul(act_one, rest_w[0]) + bias_rows[1]
    act_two = jax.nn.silu(pre_two).astype(jnp.bfloat16)
    pre_three = matmul(act_two, rest_w[1]) + bias_rows[2]
    centred = pre_three - lax.optimization_barrier(jnp.mean(pre_three, axis=-1, keepdims=True))
    inv_std = lax.rsqrt(lax.optimization_barrier(jnp.mean(centred * centred, axis=-1, keepdims=True)) + norm_eps)
    normed = centred * inv_std
    output = normed * gain_row + bias_rows[3]
    return (output, (pre_one, act_one, pre_two, act_two, normed, inv_std))

def mlp_backward(inputs, first_w, rest_w, bias_rows, gain_row, cotangent):
    _, saved = mlp_parts(inputs, first_w, rest_w, bias_rows, gain_row)
    pre_one, act_one, pre_two, act_two, normed, inv_std = saved
    grad_gain = lax.optimization_barrier(jnp.sum(cotangent * normed, axis=0))
    grad_shift = lax.optimization_barrier(jnp.sum(cotangent, axis=0))
    scaled = cotangent * gain_row
    d_three = inv_std * (scaled - lax.optimization_barrier(jnp.mean(scaled, axis=-1, keepdims=True)) - normed * lax.optimization_barrier(jnp.mean(scaled * normed, axis=-1, keepdims=True)))
    d_three_b = d_three.astype(jnp.bfloat16)
    grad_w3 = matmul_tn(act_two, d_three_b)
    d_two = matmul_nt(d_three_b, rest_w[1]) * silu_grad(pre_two)
    d_two_b = d_two.astype(jnp.bfloat16)
    grad_w2 = matmul_tn(act_one, d_two_b)
    d_one = matmul_nt(d_two_b, rest_w[0]) * silu_grad(pre_one)
    d_one_b = d_one.astype(jnp.bfloat16)
    grad_w1 = matmul_tn(inputs, d_one_b)
    grad_in = matmul_nt(d_one_b, first_w)
    bias_grads = jnp.stack([lax.optimization_barrier(jnp.sum(d_one, axis=0)), lax.optimization_barrier(jnp.sum(d_two, axis=0)), lax.optimization_barrier(jnp.sum(d_three, axis=0)), grad_shift])
    return (grad_in, (grad_w1, jnp.stack([grad_w2, grad_w3]), bias_grads, grad_gain))

def edge_messages(weights, node_latents, latents, sources, targets, keep_rows, rows):

    def one_block(block):
        block_latents, block_sources, block_targets, block_keep = block
        inputs = jnp.concatenate([block_latents, node_latents[block_sources], node_latents[block_targets]], axis=1)
        message, _ = mlp_parts(inputs, *weights)
        return message * block_keep[:, None]
    blocks = (latents.reshape(-1, rows, D), sources.reshape(-1, rows), targets.reshape(-1, rows), keep_rows.reshape(-1, rows))
    return lax.map(one_block, blocks).reshape(-1, D)

def edge_gradients(weights, node_latents, latents, sources, targets, keep_rows, cotangent, upstream_nodes, grad_nodes, rows):

    def one_block(carried, block):
        running, grad_sums = carried
        block_latents, block_sources, block_targets, block_keep, block_cot = block
        inputs = jnp.concatenate([block_latents, node_latents[block_sources], node_latents[block_targets]], axis=1)
        incoming_cot = block_cot.astype(jnp.float32)
        upstream = block_keep[:, None] * (incoming_cot + upstream_nodes[block_targets])
        in_grad, weight_grads = mlp_backward(inputs, *weights, upstream)
        running = running.at[block_sources].add(in_grad[:, D:2 * D]).at[block_targets].add(in_grad[:, 2 * D:])
        grad_sums = jax.tree.map(jnp.add, grad_sums, weight_grads)
        return ((running, grad_sums), (incoming_cot + in_grad[:, :D]).astype(jnp.bfloat16))
    empty_grads = (jnp.zeros((3 * D, D), jnp.float32), jnp.zeros((2, D, D), jnp.float32), jnp.zeros((4, D), jnp.float32), jnp.zeros((D,), jnp.float32))
    blocks = (latents.reshape(-1, rows, D), sources.reshape(-1, rows), targets.reshape(-1, rows), keep_rows.reshape(-1, rows), cotangent.reshape(-1, rows, D))
    (grad_nodes, grad_sums), own_grads = lax.scan(one_block, (grad_nodes, empty_grads), blocks)
    return (grad_nodes, grad_sums, own_grads.reshape(-1, D))

def reference(node_latents, mesh_latents, world_latents, mesh_src, mesh_dst, world_src, world_dst, send_blocks, world_count, node_cot, mesh_cot, world_cot, first_weights, rest_weights, biases, gains):
    device_count = N_DOM * N_DP
    node_count = node_latents.shape[0]
    weights = [(first_weights[which], rest_weights[which], biases[which], gains[which]) for which in range(3)]
    mesh_device = jnp.arange(mesh_src.shape[0], dtype=jnp.int32) // MEDGE_DEV
    offset = mesh_src - HALO
    neighbor_step = offset // NODE_DEV
    mesh_source = ((mesh_device + neighbor_step * N_DP) * NODE_DEV + offset - neighbor_step * NODE_DEV).astype(jnp.int32)
    mesh_target = (mesh_device * NODE_DEV + mesh_dst).astype(jnp.int32)
    mesh_keep = jnp.ones(mesh_src.shape, jnp.float32)
    world_index = jnp.arange(world_src.shape[0], dtype=jnp.int32)
    world_device = world_index // WEDGE_DEV
    peer_domain = world_src // (SLOTS * BLK)
    slot_index = world_src // BLK % SLOTS
    row_within = world_src % BLK
    owner = peer_domain * N_DP + world_device % N_DP
    chosen = send_blocks[owner, world_device // N_DP, slot_index]
    world_source = (owner * NODE_DEV + chosen * BLK + row_within).astype(jnp.int32)
    world_target = (world_device * NODE_DEV + world_dst).astype(jnp.int32)
    world_keep = (world_index % WEDGE_DEV < world_count[world_device]).astype(jnp.float32)
    mesh_message = edge_messages(weights[0], node_latents, mesh_latents, mesh_source, mesh_target, mesh_keep, MEDGE_DEV)
    world_message = edge_messages(weights[1], node_latents, world_latents, world_source, world_target, world_keep, WEDGE_DEV)
    new_mesh = (mesh_latents.astype(jnp.float32) + mesh_message).astype(jnp.bfloat16)
    new_world = (world_latents.astype(jnp.float32) + world_message).astype(jnp.bfloat16)
    mesh_sum = jax.ops.segment_sum(mesh_message, mesh_target, num_segments=node_count)
    world_sum = jax.ops.segment_sum(world_message, world_target, num_segments=node_count)
    node_input = jnp.concatenate([node_latents, mesh_sum.astype(jnp.bfloat16), world_sum.astype(jnp.bfloat16)], axis=1)
    node_update, _ = mlp_parts(node_input, *weights[2])
    new_nodes = (node_latents.astype(jnp.float32) + node_update).astype(jnp.bfloat16)
    node_back, node_grads = mlp_backward(node_input, *weights[2], node_cot.astype(jnp.float32))
    grad_nodes = node_cot.astype(jnp.float32) + node_back[:, :D]
    mesh_back = node_back[:, D:2 * D]
    world_back = node_back[:, 2 * D:]
    grad_nodes, mesh_grads, grad_mesh = edge_gradients(weights[0], node_latents, mesh_latents, mesh_source, mesh_target, mesh_keep, mesh_cot, mesh_back, grad_nodes, MEDGE_DEV)
    grad_nodes, world_grads, grad_world = edge_gradients(weights[1], node_latents, world_latents, world_source, world_target, world_keep, world_cot, world_back, grad_nodes, WEDGE_DEV)
    summed_all = [jnp.stack([mesh_grads[which], world_grads[which], node_grads[which]]) / device_count for which in range(4)]
    return (new_nodes, new_mesh, new_world, grad_nodes.astype(jnp.bfloat16), grad_mesh, grad_world, summed_all[0], summed_all[1], summed_all[2], summed_all[3])
```

```python
import functools

import jax
import jax.numpy as jnp
from jax import lax
from jax.experimental import pallas as pl
from jax.experimental.pallas import tpu as pltpu
from jax.sharding import PartitionSpec as P

D = 128
HALO = 256
BLK = 16
ROWS = 512
EPS = 1e-05
GRADS = 2048
BF = jnp.bfloat16
F32 = jnp.float32
MESH = pl.DeviceIdType.MESH


def nn(left, right):
    return jnp.dot(left, right, preferred_element_type=F32)


def nt(left, right):
    return lax.dot_general(left, right, (((1,), (1,)), ((), ())), preferred_element_type=F32)


def tn(left, right):
    return lax.dot_general(left, right, (((0,), (0,)), ((), ())), preferred_element_type=F32)


def sigma(values):
    return 0.5 + 0.5 * jnp.tanh(0.5 * values)


def lane_mean(values):
    return jnp.sum(values, axis=-1, keepdims=True) * (1.0 / D)


def pick_rows(out_ref, index_ref, first, groups, blocks):
    lane = lax.broadcasted_iota(jnp.int32, (128, 128), 1)
    for g in range(groups):
        row = index_ref[pl.ds(first + g, 1), :]
        column = jnp.transpose(jnp.broadcast_to(row, (128, 128)))
        if blocks <= 16:
            for b in range(blocks):
                hit = column == lane + b * 128
                out_ref[g * 128 : (g + 1) * 128, b * 128 : (b + 1) * 128] = jnp.where(
                    hit, 1.0, 0.0
                ).astype(BF)
        else:

            @pl.loop(0, blocks)
            def _(b):
                hit = column == lane + b * 128
                out_ref[g * 128 : (g + 1) * 128, pl.ds(pl.multiple_of(b * 128, 128), 128)] = (
                    jnp.where(hit, 1.0, 0.0).astype(BF)
                )


def pick_columns(out_ref, index_ref, first, groups, blocks):
    down = lax.broadcasted_iota(jnp.int32, (128, 128), 0)
    for g in range(groups):
        row = jnp.broadcast_to(index_ref[pl.ds(first + g, 1), :], (128, 128))
        if blocks <= 16:
            for b in range(blocks):
                hit = row == down + b * 128
                out_ref[b * 128 : (b + 1) * 128, g * 128 : (g + 1) * 128] = jnp.where(
                    hit, 1.0, 0.0
                ).astype(BF)
        else:

            @pl.loop(0, blocks)
            def _(b):
                hit = row == down + b * 128
                out_ref[pl.ds(pl.multiple_of(b * 128, 128), 128), g * 128 : (g + 1) * 128] = (
                    jnp.where(hit, 1.0, 0.0).astype(BF)
                )


def layers(which, pre_one, rest_ref, bias_ref):
    sig_one = sigma(pre_one)
    act_one = (pre_one * sig_one).astype(BF)
    pre_two = nn(act_one, rest_ref[which, 0]) + bias_ref[which, 1:2, :]
    sig_two = sigma(pre_two)
    act_two = (pre_two * sig_two).astype(BF)
    pre_three = nn(act_two, rest_ref[which, 1]) + bias_ref[which, 2:3, :]
    centred = pre_three - lane_mean(pre_three)
    inv_std = lax.rsqrt(lane_mean(centred * centred) + EPS)
    return sig_one, act_one, pre_two, sig_two, act_two, centred, inv_std


def layers_back(which, cot, pre_one, sig_one, pre_two, sig_two, normed, inv_std, rest_ref, gain_ref):
    scaled = cot * gain_ref[which : which + 1, :]
    d_three = inv_std * (scaled - lane_mean(scaled) - normed * lane_mean(scaled * normed))
    d_three_b = d_three.astype(BF)
    d_two = nt(d_three_b, rest_ref[which, 1]) * (sig_two * (1.0 + pre_two * (1.0 - sig_two)))
    d_two_b = d_two.astype(BF)
    d_one = nt(d_two_b, rest_ref[which, 0]) * (sig_one * (1.0 + pre_one * (1.0 - sig_one)))
    d_one_b = d_one.astype(BF)

    def total(values):
        return jnp.sum(values, axis=0, keepdims=True)

    sums = jnp.concatenate(
        [
            total(d_one),
            total(d_two),
            total(d_three),
            total(cot),
            total(cot * normed),
            jnp.zeros((3, D), F32),
        ],
        axis=0,
    )
    return d_one_b, d_two_b, d_three_b, sums


def prep_kernel(blocks_ref, node_ref, out_ref):
    @pl.loop(0, 512, unroll=8)
    def _(i):
        block = blocks_ref[i]
        out_ref[pl.ds(pl.multiple_of(i * BLK, BLK), BLK), :] = node_ref[
            pl.ds(pl.multiple_of(block * BLK, BLK), BLK), :
        ]


def mesh_kernel(
    src_ref, dst_ref, node_ref, before_ref, after_ref, lat_ref, first_ref, rest_ref, bias_ref,
    gain_ref, new_ref, sum_ref, one_ref, two_ref, centred_ref, pick_src, pick_dst, put_dst, total
):
    step = pl.program_id(0)
    groups = ROWS // 128
    first = step * groups
    pick_rows(pick_src, src_ref, first, groups, 12)
    pick_rows(pick_dst, dst_ref, first, groups, 8)
    pick_columns(put_dst, dst_ref, first, groups, 8)
    source = (
        nn(pick_src[:, :HALO], before_ref[...])
        + nn(pick_src[:, HALO : HALO + 1024], node_ref[...])
        + nn(pick_src[:, HALO + 1024 :], after_ref[...])
    ).astype(BF)
    target = nn(pick_dst[...], node_ref[...]).astype(BF)
    lat = lat_ref[...]
    pre_one = (
        nn(lat, first_ref[0, :D, :])
        + nn(source, first_ref[0, D : 2 * D, :])
        + nn(target, first_ref[0, 2 * D :, :])
        + bias_ref[0, 0:1, :]
    )
    _, _, pre_two, _, _, centred, inv_std = layers(0, pre_one, rest_ref, bias_ref)
    message = centred * inv_std * gain_ref[0:1, :] + bias_ref[0, 3:4, :]
    new_ref[...] = (lat.astype(F32) + message).astype(BF)
    one_ref[...] = pre_one
    two_ref[...] = pre_two
    centred_ref[...] = centred
    added = nn(put_dst[...], message.astype(BF))

    @pl.when(step == 0)
    def _():
        total[...] = added

    @pl.when(step > 0)
    def _():
        total[...] += added

    @pl.when(step == pl.num_programs(0) - 1)
    def _():
        sum_ref[...] = total[...].astype(BF)


def middle_kernel(
    count_ref, src_ref, dst_ref, node_ref, incoming_ref, lat_ref, cot_ref, sum_ref, node_cot_ref,
    first_ref, rest_ref, bias_ref, gain_ref, new_nodes_ref, new_world_ref, grad_world_ref,
    back_ref, mesh_back_ref, local_ref, world_grad_ref, node_grad_ref, small_ref, pick_src,
    pick_dst, put_src, put_dst, world_back
):
    groups = 4
    live_rows = count_ref[0]
    keep = (lax.broadcasted_iota(jnp.int32, (512, D), 0) < live_rows).astype(F32)
    pick_rows(pick_src, src_ref, 0, groups, 64)
    pick_rows(pick_dst, dst_ref, 0, groups, 8)
    pick_columns(put_dst, dst_ref, 0, groups, 8)
    source = nn(pick_src[...], incoming_ref[...]).astype(BF)
    target = nn(pick_dst[...], node_ref[...]).astype(BF)
    lat = lat_ref[...]
    inputs = jnp.concatenate([lat, source, target], axis=1)
    pre_one = nn(inputs, first_ref[1]) + bias_ref[1, 0:1, :]
    sig_one, act_one, pre_two, sig_two, act_two, centred, inv_std = layers(
        1, pre_one, rest_ref, bias_ref
    )
    normed = centred * inv_std
    message = keep * (normed * gain_ref[1:2, :] + bias_ref[1, 3:4, :])
    new_world_ref[...] = (lat.astype(F32) + message).astype(BF)
    world_sum = nn(put_dst[...], message.astype(BF)).astype(BF)

    for half in range(2):
        rows = slice(half * 512, half * 512 + 512)
        node = node_ref[rows, :]
        n_inputs = jnp.concatenate([node, sum_ref[rows, :], world_sum[rows, :]], axis=1)
        n_one = nn(n_inputs, first_ref[2]) + bias_ref[2, 0:1, :]
        n_sig_one, n_act_one, n_two, n_sig_two, n_act_two, n_centred, n_inv = layers(
            2, n_one, rest_ref, bias_ref
        )
        n_normed = n_centred * n_inv
        new_nodes_ref[rows, :] = (
            node.astype(F32) + n_normed * gain_ref[2:3, :] + bias_ref[2, 3:4, :]
        ).astype(BF)
        n_cot = node_cot_ref[rows, :].astype(F32)
        e_one, e_two, e_three, sums = layers_back(
            2, n_cot, n_one, n_sig_one, n_two, n_sig_two, n_normed, n_inv, rest_ref, gain_ref
        )
        g_first = tn(n_inputs, e_one)
        g_two = tn(n_act_one, e_two)
        g_three = tn(n_act_two, e_three)
        if half == 0:
            node_grad_ref[: 3 * D, :] = g_first
            node_grad_ref[3 * D : 4 * D, :] = g_two
            node_grad_ref[4 * D :, :] = g_three
            small_ref[8:, :] = sums
        else:
            node_grad_ref[: 3 * D, :] += g_first
            node_grad_ref[3 * D : 4 * D, :] += g_two
            node_grad_ref[4 * D :, :] += g_three
            small_ref[8:, :] += sums
        local_ref[rows, :] = n_cot + nt(e_one, first_ref[2, :D, :])
        mesh_back_ref[rows, :] = nt(e_one, first_ref[2, D : 2 * D, :]).astype(BF)
        world_back[rows, :] = nt(e_one, first_ref[2, 2 * D :, :]).astype(BF)

    own_cot = cot_ref[...].astype(F32)
    cot = keep * (own_cot + nn(pick_dst[...], world_back[...]))
    d_one, d_two, d_three, sums = layers_back(
        1, cot, pre_one, sig_one, pre_two, sig_two, normed, inv_std, rest_ref, gain_ref
    )
    small_ref[:8, :] = sums
    world_grad_ref[: 3 * D, :] = tn(inputs, d_one)
    world_grad_ref[3 * D : 4 * D, :] = tn(act_one, d_two)
    world_grad_ref[4 * D :, :] = tn(act_two, d_three)
    grad_world_ref[...] = (own_cot + nt(d_one, first_ref[1, :D, :])).astype(BF)
    to_source = nt(d_one, first_ref[1, D : 2 * D, :]).astype(BF)
    to_target = nt(d_one, first_ref[1, 2 * D :, :]).astype(BF)
    local_ref[...] += nn(put_dst[...], to_target)
    pick_columns(put_src, src_ref, 0, groups, 64)

    @pl.loop(0, 8)
    def _(b):
        rows = pl.ds(pl.multiple_of(b * 1024, 1024), 1024)
        back_ref[rows, :] = nn(put_src[rows, :], to_source).astype(BF)


def mesh_back_kernel(
    src_ref, dst_ref, node_ref, before_ref, after_ref, lat_ref, cot_ref, one_ref, two_ref,
    centred_ref, back_ref, part_ref, first_ref, rest_ref, gain_ref, grad_ref, left_ref, right_ref,
    local_ref, weight_ref, small_ref, pick_dst, put_src, put_dst, by_src, by_dst
):
    step = pl.program_id(0)
    groups = ROWS // 128
    first = step * groups
    pick_rows(pick_dst, dst_ref, first, groups, 8)
    pick_columns(put_src, src_ref, first, groups, 12)
    pick_columns(put_dst, dst_ref, first, groups, 8)
    lat = lat_ref[...]
    own_cot = cot_ref[...].astype(F32)
    cot = own_cot + nn(pick_dst[...], back_ref[...])
    pre_one = one_ref[...]
    pre_two = two_ref[...]
    centred = centred_ref[...]
    sig_one = sigma(pre_one)
    sig_two = sigma(pre_two)
    inv_std = lax.rsqrt(lane_mean(centred * centred) + EPS)
    normed = centred * inv_std
    d_one, d_two, d_three, sums = layers_back(
        0, cot, pre_one, sig_one, pre_two, sig_two, normed, inv_std, rest_ref, gain_ref
    )
    grad_ref[...] = (own_cot + nt(d_one, first_ref[0, :D, :])).astype(BF)
    g_lat = tn(lat, d_one)
    g_two = tn((pre_one * sig_one).astype(BF), d_two)
    g_three = tn((pre_two * sig_two).astype(BF), d_three)
    s_src = nn(put_src[...], d_one)
    s_dst = nn(put_dst[...], d_one)

    @pl.when(step == 0)
    def _():
        weight_ref[:D, :] = g_lat
        weight_ref[3 * D : 4 * D, :] = g_two
        weight_ref[4 * D :, :] = g_three
        small_ref[...] = sums
        by_src[...] = s_src
        by_dst[...] = s_dst

    @pl.when(step > 0)
    def _():
        weight_ref[:D, :] += g_lat
        weight_ref[3 * D : 4 * D, :] += g_two
        weight_ref[4 * D :, :] += g_three
        small_ref[...] += sums
        by_src[...] += s_src
        by_dst[...] += s_dst

    @pl.when(step == pl.num_programs(0) - 1)
    def _():
        src_sum = by_src[...].astype(BF)
        dst_sum = by_dst[...].astype(BF)
        weight_src = first_ref[0, D : 2 * D, :]
        left_ref[...] = nt(src_sum[:HALO], weight_src).astype(BF)
        right_ref[...] = nt(src_sum[HALO + 1024 :], weight_src).astype(BF)
        inner = src_sum[HALO : HALO + 1024]
        local_ref[...] = part_ref[...] + nt(inner, weight_src) + nt(dst_sum, first_ref[0, 2 * D :, :])
        weight_ref[D : 2 * D, :] = (
            tn(before_ref[...], src_sum[:HALO])
            + tn(node_ref[...], inner)
            + tn(after_ref[...], src_sum[HALO + 1024 :])
        )
        weight_ref[2 * D : 3 * D, :] = tn(node_ref[...], dst_sum)


def final_kernel(blocks_ref, part_ref, returned_ref, left_ref, right_ref, out_ref, total):
    total[...] = part_ref[...]
    total[:HALO, :] += left_ref[...].astype(F32)
    total[1024 - HALO :, :] += right_ref[...].astype(F32)

    @pl.loop(0, 512, unroll=4)
    def _(i):
        rows = pl.ds(pl.multiple_of(blocks_ref[i] * BLK, BLK), BLK)
        total[rows, :] += returned_ref[pl.ds(pl.multiple_of(i * BLK, BLK), BLK), :].astype(F32)

    out_ref[...] = total[...].astype(BF)


def reduce_kernel(
    n_dom, n_dp, mesh_ref, world_ref, node_ref, mesh_small_ref, other_small_ref, out_ref, sent,
    got, pair, sent_1, got_1, sent_2, got_2, sent_3, got_3
):
    dom = lax.axis_index("dom")
    dp = lax.axis_index("dp")
    rows = GRADS // n_dom
    barrier = pltpu.get_barrier_semaphore()

    @pl.loop(1, n_dom)
    def _(s):
        pl.semaphore_signal(
            barrier, inc=1, device_id=(lax.rem(dom + s, n_dom), dp), device_id_type=MESH
        )

    @pl.loop(1, n_dp)
    def _(s):
        pl.semaphore_signal(
            barrier, inc=1, device_id=(dom, lax.rem(dp + s, n_dp)), device_id_type=MESH
        )

    sent[:640, :] = mesh_ref[...].astype(BF)
    sent[640:1280, :] = world_ref[...].astype(BF)
    sent[1280:1920, :] = node_ref[...].astype(BF)
    sent[1920:, :] = jnp.concatenate(
        [mesh_small_ref[...], other_small_ref[...], jnp.zeros((104, D), F32)], axis=0
    ).astype(BF)
    pl.semaphore_wait(barrier, n_dom - 1 + n_dp - 1)

    def span(which):
        return pl.ds(pl.multiple_of(which * rows, rows), rows)

    def scatter(s):
        to = lax.rem(dom + s, n_dom)
        return pltpu.make_async_remote_copy(
            src_ref=sent.at[span(to)], dst_ref=got.at[span(dom)], send_sem=sent_1.at[s],
            recv_sem=got_1.at[s], device_id=(to, dp), device_id_type=MESH,
        )

    def swap(s):
        return pltpu.make_async_remote_copy(
            src_ref=pair.at[span(dp)], dst_ref=pair.at[span(dp)], send_sem=sent_2.at[s],
            recv_sem=got_2.at[s], device_id=(dom, lax.rem(dp + s, n_dp)), device_id_type=MESH,
        )

    def spread(s):
        return pltpu.make_async_remote_copy(
            src_ref=out_ref.at[span(dom)], dst_ref=out_ref.at[span(dom)], send_sem=sent_3.at[s],
            recv_sem=got_3.at[s], device_id=(lax.rem(dom + s, n_dom), dp), device_id_type=MESH,
        )

    @pl.loop(1, n_dom)
    def _(s):
        scatter(s).start()

    def collect(s, total):
        scatter(s).wait_recv()
        return total + got[span(lax.rem(dom - s + n_dom, n_dom)), :].astype(F32)

    total = lax.fori_loop(1, n_dom, collect, sent[span(dom), :].astype(F32))
    pair[span(dp), :] = total.astype(BF)
    for s in range(1, n_dp):
        swap(s).start()
    for s in range(1, n_dp):
        swap(s).wait_recv()
    total = pair[:rows, :].astype(F32)
    for i in range(1, n_dp):
        total = total + pair[i * rows : (i + 1) * rows, :].astype(F32)
    out_ref[span(dom), :] = (total * (1.0 / (n_dom * n_dp))).astype(BF)

    @pl.loop(1, n_dom)
    def _(s):
        spread(s).start()

    @pl.loop(1, n_dom)
    def _(s):
        scatter(s).wait_send()
        spread(s).wait()

    for s in range(1, n_dp):
        swap(s).wait_send()


def whole(shape):
    return pl.BlockSpec(shape, lambda i: (0,) * len(shape))


def blocked(rows):
    return pl.BlockSpec((rows, D), lambda i: (i, 0))


VMEM = pl.BlockSpec(memory_space=pltpu.VMEM)
SMEM = pl.BlockSpec(memory_space=pltpu.SMEM)
PARAMS = dict(vmem_limit_bytes=58 * 1024 * 1024)


def shape(rows, dtype):
    return jax.ShapeDtypeStruct((rows, D), dtype)


def per_device(
    node_latents,
    mesh_latents,
    world_latents,
    mesh_src,
    mesh_dst,
    world_src,
    world_dst,
    send_blocks,
    world_count,
    node_cot,
    mesh_cot,
    world_cot,
    first_weights,
    rest_weights,
    biases,
    gains,
):
    n_dom = lax.axis_size("dom")
    n_dp = lax.axis_size("dp")
    n_mesh = mesh_latents.shape[0]
    steps = n_mesh // ROWS
    up = [(i, i + 1) for i in range(n_dom - 1)]
    down = [(j, i) for i, j in up]
    blocks = send_blocks.reshape(-1)
    src = mesh_src.reshape(-1, 128)
    dst = mesh_dst.reshape(-1, 128)
    w_src = world_src.reshape(-1, 128)
    w_dst = world_dst.reshape(-1, 128)

    before = lax.ppermute(node_latents[1024 - HALO :], "dom", up)
    after = lax.ppermute(node_latents[:HALO], "dom", down)
    sending = pl.pallas_call(
        prep_kernel,
        out_shape=shape(8192, BF),
        in_specs=[SMEM, VMEM],
        out_specs=VMEM,
        cost_estimate=pl.CostEstimate(flops=0, bytes_accessed=4 << 20, transcendentals=0),
        name="prep",
    )(blocks, node_latents)
    incoming = lax.all_to_all(sending, "dom", split_axis=0, concat_axis=0, tiled=True)

    weight_specs = [
        whole((3, 3 * D, D)), whole((3, 2, D, D)), whole((3, 4, D)), whole((3, D)),
    ]
    index = whole((n_mesh // 128, 128))
    new_mesh, mesh_sum, pre_one, pre_two, centred = pl.pallas_call(
        mesh_kernel,
        grid=(steps,),
        out_shape=[shape(n_mesh, BF), shape(1024, BF)] + [shape(n_mesh, F32)] * 3,
        in_specs=[index, index, whole((1024, D)), whole((HALO, D)), whole((HALO, D)), blocked(ROWS)]
        + weight_specs,
        out_specs=[blocked(ROWS), whole((1024, D))] + [blocked(ROWS)] * 3,
        scratch_shapes=[
            pltpu.VMEM((ROWS, 1536), BF),
            pltpu.VMEM((ROWS, 1024), BF),
            pltpu.VMEM((1024, ROWS), BF),
            pltpu.VMEM((1024, D), F32),
        ],
        compiler_params=pltpu.CompilerParams(**PARAMS),
        cost_estimate=pl.CostEstimate(flops=8 << 30, bytes_accessed=8 << 20, transcendentals=1 << 20),
        name="mesh_forward",
    )(src, dst, node_latents, before, after, mesh_latents, first_weights, rest_weights, biases, gains)

    (
        new_nodes, new_world, grad_world, back, mesh_back, part, world_grad, node_grad, small
    ) = pl.pallas_call(
        middle_kernel,
        out_shape=[
            shape(1024, BF), shape(512, BF), shape(512, BF), shape(8192, BF), shape(1024, BF),
            shape(1024, F32), shape(640, F32), shape(640, F32), shape(16, F32),
        ],
        in_specs=[SMEM] + [VMEM] * 12,
        out_specs=[VMEM] * 9,
        scratch_shapes=[
            pltpu.VMEM((512, 8192), BF),
            pltpu.VMEM((512, 1024), BF),
            pltpu.VMEM((8192, 512), BF),
            pltpu.VMEM((1024, 512), BF),
            pltpu.VMEM((1024, D), BF),
        ],
        compiler_params=pltpu.CompilerParams(**PARAMS),
        cost_estimate=pl.CostEstimate(flops=4 << 30, bytes_accessed=8 << 20, transcendentals=1 << 20),
        name="world_and_nodes",
    )(
        world_count, w_src, w_dst, node_latents, incoming, world_latents, world_cot, mesh_sum,
        node_cot, first_weights, rest_weights, biases, gains,
    )
    returned = lax.all_to_all(back, "dom", split_axis=0, concat_axis=0, tiled=True)

    grad_mesh, left, right, local, mesh_grad, mesh_small = pl.pallas_call(
        mesh_back_kernel,
        grid=(steps,),
        out_shape=[
            shape(n_mesh, BF), shape(HALO, BF), shape(HALO, BF), shape(1024, F32),
            shape(640, F32), shape(8, F32),
        ],
        in_specs=[index, index, whole((1024, D)), whole((HALO, D)), whole((HALO, D))]
        + [blocked(ROWS)] * 5
        + [whole((1024, D)), whole((1024, D)), weight_specs[0], weight_specs[1], weight_specs[3]],
        out_specs=[
            blocked(ROWS), whole((HALO, D)), whole((HALO, D)), whole((1024, D)), whole((640, D)),
            whole((8, D)),
        ],
        scratch_shapes=[
            pltpu.VMEM((ROWS, 1024), BF),
            pltpu.VMEM((1536, ROWS), BF),
            pltpu.VMEM((1024, ROWS), BF),
            pltpu.VMEM((1536, D), F32),
            pltpu.VMEM((1024, D), F32),
        ],
        compiler_params=pltpu.CompilerParams(**PARAMS),
        cost_estimate=pl.CostEstimate(flops=8 << 30, bytes_accessed=8 << 20, transcendentals=1 << 20),
        name="mesh_backward",
    )(
        src, dst, node_latents, before, after, mesh_latents, mesh_cot, pre_one, pre_two, centred,
        mesh_back, part, first_weights, rest_weights, gains,
    )
    from_right = lax.ppermute(left, "dom", down)
    from_left = lax.ppermute(right, "dom", up)

    def dma(count):
        return pltpu.SemaphoreType.DMA((count,))

    packed = pl.pallas_call(
        functools.partial(reduce_kernel, n_dom, n_dp),
        out_shape=shape(GRADS, BF),
        in_specs=[VMEM] * 5,
        out_specs=VMEM,
        scratch_shapes=[
            pltpu.VMEM((GRADS, D), BF),
            pltpu.VMEM((GRADS, D), BF),
            pltpu.VMEM((n_dp * GRADS // n_dom, D), BF),
            dma(n_dom), dma(n_dom), dma(n_dp), dma(n_dp), dma(n_dom), dma(n_dom),
        ],
        compiler_params=pltpu.CompilerParams(collective_id=0, has_side_effects=True),
        name="reduce_grads",
    )(mesh_grad, world_grad, node_grad, mesh_small, small)

    grad_nodes = pl.pallas_call(
        final_kernel,
        out_shape=shape(1024, BF),
        in_specs=[SMEM] + [VMEM] * 4,
        out_specs=VMEM,
        scratch_shapes=[pltpu.VMEM((1024, D), F32)],
        name="gather_gradients",
    )(blocks, local, returned, from_left, from_right)

    big = packed[:1920].astype(F32).reshape(3, 640, D)
    tiny = packed[1920:1944].astype(F32).reshape(3, 8, D)
    return (
        new_nodes,
        new_mesh,
        new_world,
        grad_nodes,
        grad_mesh,
        grad_world,
        big[:, : 3 * D],
        big[:, 3 * D :].reshape(3, 2, D, D),
        tiny[:, :4],
        tiny[:, 4],
    )


def solution(mesh):
    part = P(("dom", "dp"))
    rows = P(("dom", "dp"), None)
    return jax.shard_map(
        per_device,
        mesh=mesh,
        in_specs=(
            rows, rows, rows, part, part, part, part, P(("dom", "dp"), None, None), part, rows,
            rows, rows, P(), P(), P(), P(),
        ),
        out_specs=(rows, rows, rows, rows, rows, rows, P(), P(), P(), P()),
        check_vma=False,
    )
```

```python
import functools

import jax
import jax.numpy as jnp
from jax import lax
from jax.experimental import pallas as pl
from jax.experimental.pallas import tpu as pltpu
from jax.sharding import PartitionSpec as P

D = 128
HALO = 256
BLK = 16
ROWS = 512
GROUPS = ROWS // 128
NODES = 1024
CAP = 48
LATE = 32
EARLY = 16
QUARTER = 320
N_LATE = 672
EPS = 1e-05
BF = jnp.bfloat16
F32 = jnp.float32
MESH = pl.DeviceIdType.MESH


def nn(left, right):
    return jnp.dot(left, right, preferred_element_type=F32)


def nt(left, right):
    return lax.dot_general(left, right, (((1,), (1,)), ((), ())), preferred_element_type=F32)


def tn(left, right):
    return lax.dot_general(left, right, (((0,), (0,)), ((), ())), preferred_element_type=F32)


def sigma(values):
    return 0.5 + 0.5 * jnp.tanh(0.5 * values)


def lane_mean(values):
    return jnp.sum(values, axis=-1, keepdims=True) * (1.0 / D)


def columns_of(index_ref, first):
    return [
        jnp.transpose(jnp.broadcast_to(index_ref[pl.ds(first + g, 1), :], (128, 128)))
        for g in range(GROUPS)
    ]


def load_columns(columns_ref, first):
    return [columns_ref[pl.ds(pl.multiple_of(first + g * 128, 128), 128), :] for g in range(GROUPS)]


def fold(index, half):
    return jnp.where(index >= half, index - half, index)


def pick(columns, half):
    lane = lax.broadcasted_iota(jnp.int32, (128, 128), 1).astype(jnp.int16)
    one = jnp.ones((128, 128), BF)
    zero = jnp.zeros((128, 128), BF)
    out = []
    for column in columns:
        low = fold(column, half).astype(jnp.int16)
        out.append(
            jnp.concatenate(
                [jnp.where(low == lane + jnp.int16(b * 128), one, zero) for b in range(half // 128)],
                axis=1,
            )
        )
    return jnp.concatenate(out, axis=0)


def put(index_ref, first, half):
    down = lax.broadcasted_iota(jnp.int32, (128, 128), 0).astype(jnp.int16)
    one = jnp.ones((128, 128), BF)
    zero = jnp.zeros((128, 128), BF)
    out = []
    for g in range(GROUPS):
        row = fold(index_ref[pl.ds(first + g, 1), :], half)
        low = jnp.broadcast_to(row, (128, 128)).astype(jnp.int16)
        out.append(
            jnp.concatenate(
                [jnp.where(low == down + jnp.int16(b * 128), one, zero) for b in range(half // 128)],
                axis=0,
            )
        )
    return jnp.concatenate(out, axis=1)


def gathered(picked, columns, half, table):
    both = nn(picked, table)
    return jnp.concatenate(
        [
            jnp.where(
                column >= half,
                both[g * 128 : (g + 1) * 128, D:],
                both[g * 128 : (g + 1) * 128, :D],
            )
            for g, column in enumerate(columns)
        ],
        axis=0,
    )


def halved(values, columns, half):
    out = []
    for g, column in enumerate(columns):
        rows = values[g * 128 : (g + 1) * 128, :]
        high = column >= half
        out.append(
            jnp.concatenate([jnp.where(high, 0.0, rows), jnp.where(high, rows, 0.0)], axis=1)
        )
    return jnp.concatenate(out, axis=0).astype(BF)


def layers(which, pre_one, rest_ref, bias_ref):
    sig_one = sigma(pre_one)
    act_one = (pre_one * sig_one).astype(BF)
    pre_two = nn(act_one, rest_ref[which, 0]) + bias_ref[which, 1:2, :]
    sig_two = sigma(pre_two)
    act_two = (pre_two * sig_two).astype(BF)
    pre_three = nn(act_two, rest_ref[which, 1]) + bias_ref[which, 2:3, :]
    centred = pre_three - lane_mean(pre_three)
    inv_std = lax.rsqrt(lane_mean(centred * centred) + EPS)
    return sig_one, act_one, pre_two, sig_two, act_two, centred, inv_std


def layers_back(which, cot, pre_one, sig_one, pre_two, sig_two, normed, inv_std, rest_ref, gain_ref):
    scaled = cot * gain_ref[which : which + 1, :]
    d_three = inv_std * (scaled - lane_mean(scaled) - normed * lane_mean(scaled * normed))
    d_three_b = d_three.astype(BF)
    d_two = nt(d_three_b, rest_ref[which, 1]) * (sig_two * (1.0 + pre_two * (1.0 - sig_two)))
    d_two_b = d_two.astype(BF)
    d_one = nt(d_two_b, rest_ref[which, 0]) * (sig_one * (1.0 + pre_one * (1.0 - sig_one)))
    d_one_b = d_one.astype(BF)

    def total(values):
        return jnp.sum(values, axis=0, keepdims=True)

    sums = jnp.concatenate(
        [
            total(d_one),
            total(d_two),
            total(d_three),
            total(cot),
            total(cot * normed),
            jnp.zeros((3, D), F32),
        ],
        axis=0,
    )
    return d_one_b, d_two_b, d_three_b, sums


def span(which, rows):
    return pl.ds(pl.multiple_of(which * rows, rows), rows)


def greet(n_dom, n_dp, dom, dp, barrier):
    @pl.loop(1, n_dom)
    def _(s):
        pl.semaphore_signal(
            barrier, inc=1, device_id=(lax.rem(dom + s, n_dom), dp), device_id_type=MESH
        )

    @pl.loop(1, n_dp)
    def _(s):
        pl.semaphore_signal(
            barrier, inc=1, device_id=(dom, lax.rem(dp + s, n_dp)), device_id_type=MESH
        )


def requests(count_ref, src_ref, slot_ref, ask_ref):
    lane = lax.broadcasted_iota(jnp.int32, (1, 128), 1)
    domain = lax.broadcasted_iota(jnp.int32, (32, 128), 0)
    live_rows = count_ref[0]
    owned, valued = [], []
    for g in range(4):
        row = src_ref[g : g + 1, :]
        live = lane + g * 128 < live_rows
        peer = jnp.where(live, row >> 8, -1)
        hit = jnp.where(jnp.broadcast_to(peer, (32, 128)) == domain, 1.0, 0.0)
        owned.append(hit)
        valued.append(hit * ((row & 255) + 1).astype(F32))
    owned = jnp.concatenate(owned, axis=1)
    valued = jnp.concatenate(valued, axis=1).astype(BF)
    earlier = lax.broadcasted_iota(jnp.int32, (512, 512), 0) < lax.broadcasted_iota(
        jnp.int32, (512, 512), 1
    )
    ahead = nn(owned.astype(BF), jnp.where(earlier, 1.0, 0.0).astype(BF))
    rank = jnp.sum(owned * ahead, axis=0, keepdims=True)
    most = jnp.max(jnp.sum(owned, axis=1, keepdims=True), axis=0, keepdims=True)
    place = lax.broadcasted_iota(jnp.int32, (128, 128), 1)
    placed = []
    for g in range(4):
        row = src_ref[g : g + 1, :]
        order = rank[:, g * 128 : (g + 1) * 128].astype(jnp.int32)
        fits = jnp.logical_and(lane + g * 128 < live_rows, order < CAP)
        slot_ref[g : g + 1, :] = jnp.where(fits, (row >> 8) * CAP + order, -1)
        column = jnp.transpose(jnp.broadcast_to(order, (128, 128)))
        placed.append(jnp.where(column == place, 1.0, 0.0).astype(BF))
    table = nn(valued, jnp.concatenate(placed, axis=0))
    wide = lax.broadcasted_iota(jnp.int32, (32, 128), 1)
    table = jnp.where(wide < CAP, table, 0.0)
    table = jnp.where(wide == 127, jnp.broadcast_to(most, (32, 128)), table).astype(jnp.int32)
    for p in range(32):
        ask_ref[p] = jnp.broadcast_to(table[p : p + 1, :], (8, 128))


def asked_rows(asked_ref, blocks_ref, need_ref):
    table = jnp.concatenate([asked_ref[k, 0:1, :] for k in range(32)], axis=0)
    most = jnp.max(table[:, 127:128], axis=0, keepdims=True)
    wanted = table - 1
    slot = wanted >> 4
    inside = wanted & 15
    eye = lax.broadcasted_iota(jnp.int32, (16, 128), 0) == lax.broadcasted_iota(
        jnp.int32, (16, 128), 1
    )
    blocks = tn(
        blocks_ref[...].astype(F32).astype(BF), jnp.where(eye, 1.0, 0.0).astype(BF)
    ).astype(jnp.int32)
    rows = jnp.full((32, 128), -1, jnp.int32)
    for t in range(16):
        rows = jnp.where(slot == t, blocks[:, t : t + 1] * BLK + inside, rows)
    rolled = {}
    lane = lax.broadcasted_iota(jnp.int32, (1, 128), 1)
    for g in range(32 * CAP // 128):
        line = jnp.full((1, 128), -1, jnp.int32)
        for k in range(32):
            start = k * CAP - g * 128
            if -CAP < start < 128:
                if start % 128 not in rolled:
                    rolled[start % 128] = pltpu.roll(rows, start % 128, 1) if start % 128 else rows
                piece = rolled[start % 128][k : k + 1, :]
                inside_piece = jnp.logical_and(lane >= start, lane < start + CAP)
                line = jnp.where(inside_piece, piece, line)
        need_ref[g : g + 1, :] = line
    return most


def extended(value, sides, width):
    for axis, dim in sides:
        devices, length = (lax.axis_size(axis), value.shape[dim])
        up = [(i, (i + 1) % devices) for i in range(devices - 1)]
        down = [(j, i) for i, j in up]
        last = lax.slice_in_dim(value, length - width, length, axis=dim)
        leading = lax.slice_in_dim(value, 0, width, axis=dim)
        before = lax.ppermute(last, axis, up)
        after = lax.ppermute(leading, axis, down)
        value = jnp.concatenate([before, value, after], axis=dim)
    return value


def from_behind(value, axis, steps):
    count = lax.axis_size(axis)
    leading, last = (max(0, -steps), min(count, count - steps))
    return lax.ppermute(value, axis, [(source, source + steps) for source in range(leading, last)])


def matmul(left, right):
    return jnp.dot(left, right, preferred_element_type=jnp.float32)


def matmul_nt(left, right):
    return lax.dot_general(
        left, right, (((1,), (1,)), ((), ())), preferred_element_type=jnp.float32
    )


def matmul_tn(left, right):
    return lax.dot_general(
        left, right, (((0,), (0,)), ((), ())), preferred_element_type=jnp.float32
    )


def silu_grad(values):
    sigma = jax.nn.sigmoid(values)
    return sigma * (1.0 + values * (1.0 - sigma))


def mlp_parts(inputs, first_w, rest_w, bias_rows, gain_row):
    pre_one = matmul(inputs, first_w) + bias_rows[0]
    act_one = jax.nn.silu(pre_one).astype(jnp.bfloat16)
    pre_two = matmul(act_one, rest_w[0]) + bias_rows[1]
    act_two = jax.nn.silu(pre_two).astype(jnp.bfloat16)
    pre_three = matmul(act_two, rest_w[1]) + bias_rows[2]
    centred = pre_three - jnp.mean(pre_three, axis=-1, keepdims=True)
    inv_std = lax.rsqrt(jnp.mean(centred * centred, axis=-1, keepdims=True) + EPS)
    normed = centred * inv_std
    output = normed * gain_row + bias_rows[3]
    return (output, (pre_one, act_one, pre_two, act_two, normed, inv_std))


def mlp_backward(inputs, first_w, rest_w, bias_rows, gain_row, cotangent):
    _, saved = mlp_parts(inputs, first_w, rest_w, bias_rows, gain_row)
    pre_one, act_one, pre_two, act_two, normed, inv_std = saved
    grad_gain = jnp.sum(cotangent * normed, axis=0)
    grad_shift = jnp.sum(cotangent, axis=0)
    scaled = cotangent * gain_row
    d_three = inv_std * (
        scaled
        - jnp.mean(scaled, axis=-1, keepdims=True)
        - normed * jnp.mean(scaled * normed, axis=-1, keepdims=True)
    )
    d_three_b = d_three.astype(jnp.bfloat16)
    grad_w3 = matmul_tn(act_two, d_three_b)
    d_two = matmul_nt(d_three_b, rest_w[1]) * silu_grad(pre_two)
    d_two_b = d_two.astype(jnp.bfloat16)
    grad_w2 = matmul_tn(act_one, d_two_b)
    d_one = matmul_nt(d_two_b, rest_w[0]) * silu_grad(pre_one)
    d_one_b = d_one.astype(jnp.bfloat16)
    grad_w1 = matmul_tn(inputs, d_one_b)
    grad_in = matmul_nt(d_one_b, first_w)
    bias_grads = jnp.stack(
        [jnp.sum(d_one, axis=0), jnp.sum(d_two, axis=0), jnp.sum(d_three, axis=0), grad_shift]
    )
    return (grad_in, (grad_w1, jnp.stack([grad_w2, grad_w3]), bias_grads, grad_gain))


def full_exchange(
    node_latents,
    mesh_latents,
    world_latents,
    mesh_src,
    mesh_dst,
    world_src,
    world_dst,
    send_blocks,
    world_count,
    node_cot,
    mesh_cot,
    world_cot,
    first_weights,
    rest_weights,
    biases,
    gains,
):
    node_count = node_latents.shape[0]
    latent_width = node_latents.shape[1]
    weights = [
        (first_weights[which], rest_weights[which], biases[which], gains[which])
        for which in range(3)
    ]
    padded = extended(node_latents, (("dom", 0),), HALO)
    send_index = (send_blocks[0][:, :, None] * BLK + jnp.arange(BLK, dtype=jnp.int32)).reshape(-1)
    incoming = lax.all_to_all(
        node_latents[send_index], "dom", split_axis=0, concat_axis=0, tiled=True
    )
    recv_rows = incoming.shape[0]
    mesh_inputs = jnp.concatenate([mesh_latents, padded[mesh_src], node_latents[mesh_dst]], axis=1)
    mesh_message, _ = mlp_parts(mesh_inputs, *weights[0])
    new_mesh = (mesh_latents.astype(jnp.float32) + mesh_message).astype(jnp.bfloat16)
    mesh_total = jax.ops.segment_sum(mesh_message, mesh_dst, num_segments=node_count)
    world_total_rows = world_latents.shape[0]
    live_rows = world_count[0]

    def world_inputs(row_count):
        keep_rows = (jnp.arange(row_count, dtype=jnp.int32) < live_rows).astype(jnp.float32)[
            :, None
        ]
        inputs = jnp.concatenate(
            [world_latents, incoming[world_src], node_latents[world_dst]], axis=1
        )
        return (world_latents, world_src, world_dst, keep_rows, inputs)

    latents, sources, targets, keep_rows, inputs = world_inputs(world_total_rows)
    message = mlp_parts(inputs, *weights[1])[0] * keep_rows
    updated = (latents.astype(jnp.float32) + message).astype(jnp.bfloat16)
    world_total = jax.ops.segment_sum(message, targets, num_segments=node_count)
    node_input = jnp.concatenate(
        [node_latents, mesh_total.astype(jnp.bfloat16), world_total.astype(jnp.bfloat16)], axis=1
    )
    node_update, _ = mlp_parts(node_input, *weights[2])
    new_nodes = (node_latents.astype(jnp.float32) + node_update).astype(jnp.bfloat16)
    node_back, node_grads = mlp_backward(node_input, *weights[2], node_cot.astype(jnp.float32))
    grad_local = node_cot.astype(jnp.float32) + node_back[:, :latent_width]
    mesh_back = node_back[:, latent_width : 2 * latent_width]
    world_back = node_back[:, 2 * latent_width :]
    mesh_upstream = mesh_cot.astype(jnp.float32) + mesh_back[mesh_dst]
    mesh_in_grad, mesh_grads = mlp_backward(mesh_inputs, *weights[0], mesh_upstream)
    grad_mesh = (mesh_cot.astype(jnp.float32) + mesh_in_grad[:, :latent_width]).astype(jnp.bfloat16)
    padded_grad = jax.ops.segment_sum(
        mesh_in_grad[:, latent_width : 2 * latent_width],
        mesh_src,
        num_segments=node_count + 2 * HALO,
    )
    from_right = from_behind(padded_grad[:HALO].astype(jnp.bfloat16), "dom", -1).astype(jnp.float32)
    from_left = from_behind(padded_grad[HALO + node_count :].astype(jnp.bfloat16), "dom", 1).astype(
        jnp.float32
    )
    grad_local = grad_local + padded_grad[HALO : HALO + node_count]
    grad_local = grad_local + jax.ops.segment_sum(
        mesh_in_grad[:, 2 * latent_width :], mesh_dst, num_segments=node_count
    )
    grad_local = grad_local + jnp.pad(from_left, ((0, node_count - HALO), (0, 0)))
    grad_local = grad_local + jnp.pad(from_right, ((node_count - HALO, 0), (0, 0)))
    latents, sources, targets, keep_rows, inputs = world_inputs(world_total_rows)
    cotangent = world_cot.astype(jnp.float32)
    in_grad, weight_grads = mlp_backward(
        inputs, *weights[1], keep_rows * (cotangent + world_back[targets])
    )
    own_grad = (cotangent + in_grad[:, :latent_width]).astype(jnp.bfloat16)
    to_source = jax.ops.segment_sum(
        in_grad[:, latent_width : 2 * latent_width], sources, num_segments=recv_rows
    )
    to_target = jax.ops.segment_sum(
        in_grad[:, 2 * latent_width :], targets, num_segments=node_count
    )
    returned = lax.all_to_all(
        to_source.astype(jnp.bfloat16), "dom", split_axis=0, concat_axis=0, tiled=True
    ).astype(to_source.dtype)
    grad_local = (
        grad_local + to_target + jax.ops.segment_sum(returned, send_index, num_segments=node_count)
    )
    grad_nodes = grad_local.astype(jnp.bfloat16)
    packed = jnp.concatenate(
        [
            jnp.stack([mesh_grads[0], weight_grads[0], node_grads[0]]).reshape(-1, latent_width),
            jnp.stack([mesh_grads[1], weight_grads[1], node_grads[1]]).reshape(-1, latent_width),
            jnp.stack([mesh_grads[2], weight_grads[2], node_grads[2]]).reshape(-1, latent_width),
            jnp.stack([mesh_grads[3], weight_grads[3], node_grads[3]]),
        ]
    )
    devices = lax.axis_size("dom") * lax.axis_size("dp")
    used = packed.shape[0]
    packed = jnp.pad(packed, ((0, -used % (8 * devices)), (0, 0)))
    everyone = ("dom", "dp")
    pieces = lax.all_to_all(packed, everyone, split_axis=0, concat_axis=0, tiled=True)
    piece = jnp.sum(pieces.reshape(devices, -1, latent_width), axis=0) / devices
    total = lax.all_to_all(
        jnp.tile(piece, (devices, 1)), everyone, split_axis=0, concat_axis=0, tiled=True
    )
    first_rows = 9 * latent_width
    rest_rows = first_rows + 6 * latent_width
    return (
        new_nodes,
        new_mesh,
        updated,
        grad_nodes,
        grad_mesh,
        own_grad,
        total[:first_rows].reshape(3, 3 * latent_width, latent_width),
        total[first_rows:rest_rows].reshape(3, 2, latent_width, latent_width),
        total[rest_rows : rest_rows + 12].reshape(3, 4, latent_width),
        total[rest_rows + 12 : used],
    )


def cloth_kernel(
    n_dom, n_dp, count_ref, wsrc_ref, wdst_ref, blocks_ref, src_ref, dst_ref, node_ref,
    node_cot_ref, wlat_ref, wcot_ref, first_ref, rest_ref, bias_ref, gain_ref, lat_hbm, cot_hbm,
    new_nodes_ref, new_world_ref, grad_nodes_ref, grad_world_ref, early_out, late_out, most_ref,
    new_mesh_hbm, grad_mesh_hbm, lat_ref, cot_ref, new_ref, grad_ref, source_ref, target_ref,
    one_ref, two_ref, centred_ref, d_ref, col_src, col_dst, col_need, pick_dst, put_dst, node2,
    ext2, back2, world_back2, got_ref, got2, before_ref, after_ref, slot_ref, need_ref, ask_ref,
    asked_ref, reply_ref, high_ref, acc_dst, acc_src, part2, weight_ref, sums_ref, sent_ref,
    returned_ref, left_ref, right_ref, from_left_ref, from_right_ref, early, early_got, early_mid,
    early_mid_got, tiny_ref, late, late_got, late_pair, in_s, out_s, ask_s, ask_r, reply_s, reply_r, halo_s, halo_r, high_s,
    high_r, back_s, back_r, rim_s, rim_r, a_s, a_r, b_s, b_r, c_s, c_r, d_s,
    d_r, e_s, e_r, f_s, f_r, g_s, g_r
):
    dom = lax.axis_index("dom")
    dp = lax.axis_index("dp")
    steps = lat_ref.shape[0] // ROWS
    half = NODES // 2
    wide = 768
    slots = CAP * n_dom // 2
    scale = 1.0 / (n_dom * n_dp)
    barrier = pltpu.get_barrier_semaphore()
    greet(n_dom, n_dp, dom, dp, barrier)
    lat_in = pltpu.make_async_copy(lat_hbm, lat_ref, in_s.at[0])
    cot_in = pltpu.make_async_copy(cot_hbm, cot_ref, in_s.at[1])
    lat_in.start()
    cot_in.start()
    requests(count_ref, wsrc_ref, slot_ref, ask_ref)
    pl.semaphore_wait(barrier, n_dom - 1 + n_dp - 1)

    def new_out(c):
        rows = span(c, ROWS)
        return pltpu.make_async_copy(new_ref.at[rows], new_mesh_hbm.at[rows], out_s.at[0, c])

    def grad_out(c):
        rows = span(c, ROWS)
        return pltpu.make_async_copy(grad_ref.at[rows], grad_mesh_hbm.at[rows], out_s.at[1, c])

    def to_domain(from_ref, to_ref, sems, semr, s):
        to = lax.rem(dom + s, n_dom)
        return pltpu.make_async_remote_copy(
            src_ref=from_ref(to), dst_ref=to_ref(dom), send_sem=sems.at[s], recv_sem=semr.at[s],
            device_id=(to, dp), device_id_type=MESH,
        )

    def ask(s):
        return to_domain(lambda to: ask_ref.at[to], lambda me: asked_ref.at[me], ask_s, ask_r, s)

    def reply(s):
        return to_domain(
            lambda to: reply_ref.at[span(to, CAP)], lambda me: got_ref.at[span(me, CAP)],
            reply_s, reply_r, s,
        )

    def give_back(s):
        return to_domain(
            lambda to: sent_ref.at[span(to, CAP)], lambda me: returned_ref.at[span(me, CAP)],
            back_s, back_r, s,
        )

    def scatter(rows, mine, got, sems, semr, s):
        return to_domain(
            lambda to: mine.at[span(lax.rem(to, mine.shape[0] // rows), rows)],
            lambda me: got.at[span(me, rows)], sems, semr, s,
        )

    def spread(rows, out, sems, semr, s):
        at = span(lax.rem(dom, out.shape[0] // rows), rows)
        return to_domain(lambda to: out.at[at], lambda me: out.at[at], sems, semr, s)

    def swap(pair, sems, semr, s):
        return pltpu.make_async_remote_copy(
            src_ref=pair.at[dp], dst_ref=pair.at[dp], send_sem=sems.at[s], recv_sem=semr.at[s],
            device_id=(dom, lax.rem(dp + s, n_dp)), device_id_type=MESH,
        )

    def neighbour(from_ref, to_ref, sems, semr, at, step):
        return pltpu.make_async_remote_copy(
            src_ref=from_ref, dst_ref=to_ref, send_sem=sems.at[at], recv_sem=semr.at[at],
            device_id=(lax.rem(dom + step, n_dom), dp), device_id_type=MESH,
        )

    def collected(rows, mine, got, sems, semr):
        def add(s, total):
            scatter(rows, mine, got, sems, semr, s).wait_recv()
            return total + got[span(lax.rem(dom - s + n_dom, n_dom), rows), :].astype(F32)

        return lax.fori_loop(1, n_dom, add, mine[span(dom, rows), :].astype(F32))

    def quarter(s):
        to = lax.rem(dp + s, n_dp)
        return pltpu.make_async_remote_copy(
            src_ref=early.at[span(to, QUARTER)], dst_ref=early_got.at[span(dp, QUARTER)],
            send_sem=a_s.at[s], recv_sem=a_r.at[s], device_id=(dom, to), device_id_type=MESH,
        )

    def middle(s):
        return scatter(EARLY, early_mid, early_mid_got, b_s, b_r, s)

    def mine():
        return pl.ds(pl.multiple_of(dp * QUARTER + lax.rem(dom, QUARTER // EARLY) * EARLY, EARLY), EARLY)

    def ready(s):
        return to_domain(
            lambda to: early_out.at[mine()], lambda me: early_out.at[mine()], c_s, c_r, s
        )

    def quarters(s):
        rows = span(dp, QUARTER)
        return pltpu.make_async_remote_copy(
            src_ref=early_out.at[rows], dst_ref=early_out.at[rows], send_sem=g_s.at[s],
            recv_sem=g_r.at[s], device_id=(dom, lax.rem(dp + s, n_dp)), device_id_type=MESH,
        )

    def paired(pair, sems, semr):
        for s in range(1, n_dp):
            swap(pair, sems, semr, s).wait_recv()
        total = pair[0]
        for i in range(1, n_dp):
            total = total + pair[i]
        return (total * scale).astype(BF)

    halo_up = neighbour(
        node_ref.at[pl.ds(NODES - HALO, HALO)], before_ref, halo_s, halo_r, 0, 1
    )
    halo_down = neighbour(node_ref.at[pl.ds(0, HALO)], after_ref, halo_s, halo_r, 1, n_dom - 1)


    @pl.loop(1, n_dom)
    def _(s):
        ask(s).start()

    halo_up.start()
    halo_down.start()
    asked_ref[dom] = ask_ref[dom]
    node2[:, :D] = node_ref[:half, :]
    node2[:, D:] = node_ref[half:, :]
    ext2[HALO:, :D] = node_ref[:half, :]
    ext2[:half, D:] = node_ref[half:, :]
    acc_dst[...] = jnp.zeros(acc_dst.shape, F32)

    @pl.loop(0, steps)
    def _(c):
        columns = columns_of(dst_ref, c * GROUPS)
        rows = span(c, ROWS)
        col_dst[rows, :] = jnp.concatenate(columns, axis=0)
        picked = pick(columns, half)
        pick_dst[rows, :] = picked
        target_ref[rows, :] = gathered(picked, columns, half, node2[...]).astype(BF)

    @pl.loop(1, n_dom)
    def _(s):
        ask(s).wait_recv()

    high_ref[dp] = jnp.broadcast_to(asked_rows(asked_ref, blocks_ref, need_ref), (8, 128))
    for s in range(1, n_dp):
        swap(high_ref, high_s, high_r, s).start()

    @pl.loop(0, need_ref.shape[0] // GROUPS)
    def _(c):
        columns = columns_of(need_ref, c * GROUPS)
        rows = span(c, ROWS)
        col_need[rows, :] = jnp.concatenate(columns, axis=0)
        reply_ref[rows, :] = gathered(pick(columns, half), columns, half, node2[...]).astype(BF)

    @pl.loop(1, n_dom)
    def _(s):
        reply(s).start()

    got_ref[span(dom, CAP), :] = reply_ref[span(dom, CAP), :]
    halo_up.wait_recv()
    halo_down.wait_recv()
    ext2[:HALO, :D] = before_ref[...]
    ext2[half:, D:] = after_ref[...]
    lat_in.wait()


    @pl.loop(0, steps)
    def _(c):
        rows = span(c, ROWS)
        columns = columns_of(src_ref, c * GROUPS)
        col_src[rows, :] = jnp.concatenate(columns, axis=0)
        source = gathered(pick(columns, wide), columns, wide, ext2[...]).astype(BF)
        source_ref[rows, :] = source
        lat = lat_ref[rows, :]
        inputs = jnp.concatenate([lat, source, target_ref[rows, :]], axis=1)
        pre_one = nn(inputs, first_ref[0]) + bias_ref[0, 0:1, :]
        _, _, pre_two, _, _, centred, inv_std = layers(0, pre_one, rest_ref, bias_ref)
        message = centred * inv_std * gain_ref[0:1, :] + bias_ref[0, 3:4, :]
        new_ref[rows, :] = (lat.astype(F32) + message).astype(BF)
        new_out(c).start()
        one_ref[rows, :] = pre_one
        two_ref[rows, :] = pre_two
        centred_ref[rows, :] = centred
        spot = put(dst_ref, c * GROUPS, half)
        put_dst[c] = spot
        acc_dst[...] += nn(spot, halved(message, load_columns(col_dst, c * ROWS), half))

    @pl.loop(1, n_dom)
    def _(s):
        reply(s).wait_recv()


    got2[:, :D] = got_ref[:slots, :]
    got2[:, D:] = got_ref[slots:, :]
    live_rows = count_ref[0]
    keep = (lax.broadcasted_iota(jnp.int32, (512, D), 0) < live_rows).astype(F32)
    slot_columns = columns_of(slot_ref, 0)
    world_columns = columns_of(wdst_ref, 0)
    world_pick = pick(world_columns, half)
    world_put = put(wdst_ref, 0, half)
    lat = wlat_ref[...]
    inputs = jnp.concatenate(
        [
            lat,
            gathered(pick(slot_columns, slots), slot_columns, slots, got2[...]).astype(BF),
            gathered(world_pick, world_columns, half, node2[...]).astype(BF),
        ],
        axis=1,
    )
    pre_one = nn(inputs, first_ref[1]) + bias_ref[1, 0:1, :]
    sig_one, act_one, pre_two, sig_two, act_two, centred, inv_std = layers(
        1, pre_one, rest_ref, bias_ref
    )
    normed = centred * inv_std
    message = keep * (normed * gain_ref[1:2, :] + bias_ref[1, 3:4, :])
    new_world_ref[...] = (lat.astype(F32) + message).astype(BF)
    world_sum = nn(world_put, halved(message, world_columns, half)).astype(BF)

    for h in range(2):
        rows = slice(h * half, h * half + half)
        side = slice(h * D, h * D + D)
        node = node_ref[rows, :]
        n_inputs = jnp.concatenate([node, acc_dst[:, side].astype(BF), world_sum[:, side]], axis=1)
        n_one = nn(n_inputs, first_ref[2]) + bias_ref[2, 0:1, :]
        n_sig_one, n_act_one, n_two, n_sig_two, n_act_two, n_centred, n_inv = layers(
            2, n_one, rest_ref, bias_ref
        )
        n_normed = n_centred * n_inv
        new_nodes_ref[rows, :] = (
            node.astype(F32) + n_normed * gain_ref[2:3, :] + bias_ref[2, 3:4, :]
        ).astype(BF)
        n_cot = node_cot_ref[rows, :].astype(F32)
        e_one, e_two, e_three, sums = layers_back(
            2, n_cot, n_one, n_sig_one, n_two, n_sig_two, n_normed, n_inv, rest_ref, gain_ref
        )
        if h == 0:
            weight_ref[: 3 * D, :] = tn(n_inputs, e_one)
            weight_ref[3 * D : 4 * D, :] = tn(n_act_one, e_two)
            weight_ref[4 * D :, :] = tn(n_act_two, e_three)
            sums_ref[...] = sums
        else:
            weight_ref[: 3 * D, :] += tn(n_inputs, e_one)
            weight_ref[3 * D : 4 * D, :] += tn(n_act_one, e_two)
            weight_ref[4 * D :, :] += tn(n_act_two, e_three)
            sums_ref[...] += sums
        part2[:, side] = n_cot + nt(e_one, first_ref[2, :D, :])
        back2[:, side] = nt(e_one, first_ref[2, D : 2 * D, :]).astype(BF)
        world_back2[:, side] = nt(e_one, first_ref[2, 2 * D :, :]).astype(BF)

    own_cot = wcot_ref[...].astype(F32)
    cot = keep * (own_cot + gathered(world_pick, world_columns, half, world_back2[...]))
    d_one, d_two, d_three, sums = layers_back(
        1, cot, pre_one, sig_one, pre_two, sig_two, normed, inv_std, rest_ref, gain_ref
    )
    to_source = nt(d_one, first_ref[1, D : 2 * D, :])
    placed = nn(put(slot_ref, 0, slots), halved(to_source, slot_columns, slots)).astype(BF)
    sent_ref[:slots, :] = placed[:, :D]
    sent_ref[slots:, :] = placed[:, D:]

    early[: 3 * D, :] = tn(inputs, d_one).astype(BF)
    early[3 * D : 4 * D, :] = tn(act_one, d_two).astype(BF)
    early[4 * D : 640, :] = tn(act_two, d_three).astype(BF)
    early[640:1280, :] = weight_ref[...].astype(BF)
    tiny_ref[:8, :] = sums
    tiny_ref[8:, :] = sums_ref[...]
    for s in range(1, n_dp):
        quarter(s).start()

    @pl.loop(1, n_dom)
    def _(s):
        give_back(s).start()

    returned_ref[span(dom, CAP), :] = sent_ref[span(dom, CAP), :]
    grad_world_ref[...] = (own_cot + nt(d_one, first_ref[1, :D, :])).astype(BF)
    to_target = nt(d_one, first_ref[1, 2 * D :, :])
    part2[...] += nn(world_put, halved(to_target, world_columns, half))


    weight_ref[...] = jnp.zeros(weight_ref.shape, F32)
    sums_ref[...] = jnp.zeros(sums_ref.shape, F32)
    acc_dst[...] = jnp.zeros(acc_dst.shape, F32)
    acc_src[...] = jnp.zeros(acc_src.shape, F32)
    cot_in.wait()

    def chunk(c, carry):
        rows = span(c, ROWS)
        own = cot_ref[rows, :].astype(F32)
        columns = load_columns(col_dst, c * ROWS)
        cot = own + gathered(pick_dst[rows, :], columns, half, back2[...])
        pre_one = one_ref[rows, :]
        pre_two = two_ref[rows, :]
        centred = centred_ref[rows, :]
        sig_one = sigma(pre_one)
        sig_two = sigma(pre_two)
        inv_std = lax.rsqrt(lane_mean(centred * centred) + EPS)
        normed = centred * inv_std
        d_one, d_two, d_three, sums = layers_back(
            0, cot, pre_one, sig_one, pre_two, sig_two, normed, inv_std, rest_ref, gain_ref
        )
        d_ref[rows, :] = d_one
        grad_ref[rows, :] = (own + nt(d_one, first_ref[0, :D, :])).astype(BF)
        grad_out(c).start()
        weight_ref[:D, :] += tn(lat_ref[rows, :], d_one)
        weight_ref[D : 2 * D, :] += tn(source_ref[rows, :], d_one)
        weight_ref[2 * D : 3 * D, :] += tn(target_ref[rows, :], d_one)
        weight_ref[3 * D : 4 * D, :] += tn((pre_one * sig_one).astype(BF), d_two)
        weight_ref[4 * D :, :] += tn((pre_two * sig_two).astype(BF), d_three)
        sums_ref[...] += sums
        return carry

    n_early = QUARTER // EARLY
    lax.fori_loop(0, steps // 3, chunk, 0)

    total = early[span(dp, QUARTER), :].astype(F32)
    for s in range(1, n_dp):
        quarter(s).wait_recv()
        total = total + early_got[span(lax.rem(dp - s + n_dp, n_dp), QUARTER), :].astype(F32)
    early_mid[...] = total

    @pl.loop(1, n_dom)
    def _(s):
        @pl.when(lax.rem(dom + s, n_dom) < n_early)
        def _():
            middle(s).start()

    lax.fori_loop(steps // 3, 2 * steps // 3, chunk, 0)

    @pl.when(dom < n_early)
    def _():
        total = collected(EARLY, early_mid, early_mid_got, b_s, b_r)
        early_out[mine(), :] = (total * scale).astype(BF)

        @pl.loop(1, n_dom)
        def _(s):
            ready(s).start()

    lax.fori_loop(2 * steps // 3, steps, chunk, 0)

    late[:640, :] = weight_ref[...].astype(BF)
    late[640:, :] = jnp.concatenate(
        [sums_ref[...], tiny_ref[...], jnp.zeros((N_LATE - 664, D), F32)], axis=0
    ).astype(BF)
    n_late = N_LATE // LATE

    @pl.loop(1, n_dom)
    def _(s):
        @pl.when(lax.rem(dom + s, n_dom) < n_late)
        def _():
            scatter(LATE, late, late_got, d_s, d_r, s).start()

    @pl.loop(1, n_dom)
    def _(s):
        @pl.when(lax.rem(dom - s + n_dom, n_dom) < n_early)
        def _():
            ready(s).wait_recv()

    for s in range(1, n_dp):
        quarters(s).start()


    @pl.loop(0, steps)
    def _(c):
        columns = load_columns(col_src, c * ROWS)
        values = d_ref[span(c, ROWS), :].astype(F32)
        acc_src[...] += nn(put(src_ref, c * GROUPS, wide), halved(values, columns, wide))

    weight_src = first_ref[0, D : 2 * D, :]
    left_ref[...] = nt(acc_src[:HALO, :D].astype(BF), weight_src).astype(BF)
    right_ref[...] = nt(acc_src[half:, D:].astype(BF), weight_src).astype(BF)
    rim_down = neighbour(left_ref, from_right_ref, rim_s, rim_r, 0, n_dom - 1)
    rim_up = neighbour(right_ref, from_left_ref, rim_s, rim_r, 1, 1)
    rim_down.start()
    rim_up.start()

    @pl.when(dom < n_late)
    def _():
        late_pair[dp] = collected(LATE, late, late_got, d_s, d_r)
        for s in range(1, n_dp):
            swap(late_pair, e_s, e_r, s).start()

    @pl.loop(0, steps)
    def _(c):
        columns = load_columns(col_dst, c * ROWS)
        values = d_ref[span(c, ROWS), :].astype(F32)
        acc_dst[...] += nn(put_dst[c], halved(values, columns, half))

    @pl.when(dom < n_late)
    def _():
        late_out[span(dom, LATE), :] = paired(late_pair, e_s, e_r)

        @pl.loop(1, n_dom)
        def _(s):
            spread(LATE, late_out, f_s, f_r, s).start()

    for h in range(2):
        side = slice(h * D, h * D + D)
        inner = acc_src[HALO:, :D] if h == 0 else acc_src[:half, D:]
        part2[:, side] += nt(inner.astype(BF), weight_src) + nt(
            acc_dst[:, side].astype(BF), first_ref[0, 2 * D :, :]
        )

    @pl.loop(1, n_dom)
    def _(s):
        give_back(s).wait_recv()

    @pl.loop(0, need_ref.shape[0] // GROUPS)
    def _(c):
        columns = load_columns(col_need, c * ROWS)
        values = returned_ref[span(c, ROWS), :].astype(F32)
        part2[...] += nn(put(need_ref, c * GROUPS, half), halved(values, columns, half))

    rim_down.wait()
    rim_up.wait()
    part2[:HALO, :D] += from_left_ref[...].astype(F32)
    part2[half - HALO :, D:] += from_right_ref[...].astype(F32)
    grad_nodes_ref[:half, :] = part2[:, :D].astype(BF)
    grad_nodes_ref[half:, :] = part2[:, D:].astype(BF)

    for s in range(1, n_dp):
        swap(high_ref, high_s, high_r, s).wait()
        quarter(s).wait_send()
        quarters(s).wait()
    high = high_ref[0]
    for i in range(1, n_dp):
        high = jnp.maximum(high, high_ref[i])
    most_ref[0] = jnp.max(high)
    halo_up.wait_send()
    halo_down.wait_send()

    @pl.loop(0, steps)
    def _(c):
        new_out(c).wait()
        grad_out(c).wait()

    @pl.loop(1, n_dom)
    def _(s):
        ask(s).wait_send()
        reply(s).wait_send()
        give_back(s).wait_send()

        @pl.when(lax.rem(dom + s, n_dom) < n_early)
        def _():
            middle(s).wait_send()

        @pl.when(dom < n_early)
        def _():
            ready(s).wait_send()

        @pl.when(lax.rem(dom + s, n_dom) < n_late)
        def _():
            scatter(LATE, late, late_got, d_s, d_r, s).wait_send()

        @pl.when(dom < n_late)
        def _():
            spread(LATE, late_out, f_s, f_r, s).wait_send()

        @pl.when(lax.rem(dom - s + n_dom, n_dom) < n_late)
        def _():
            spread(LATE, late_out, f_s, f_r, s).wait_recv()

    @pl.when(dom < n_late)
    def _():
        for s in range(1, n_dp):
            swap(late_pair, e_s, e_r, s).wait_send()


def finish_kernel(*refs):
    sources, targets, held = refs[:8], refs[8:18], refs[18:30]
    in_s, out_s = refs[30:]
    early_ref, late_ref = held[:2]
    weights = held[8:]
    first_ref, rest_ref, bias_ref, gain_ref = weights
    taken = [pltpu.make_async_copy(sources[i], held[i], in_s.at[i]) for i in range(8)]
    given = [
        pltpu.make_async_copy(from_ref, targets[i], out_s.at[i])
        for i, from_ref in enumerate(list(held[2:8]) + list(weights))
    ]
    for copy in taken:
        copy.start()
    taken[0].wait()
    taken[1].wait()
    small = late_ref[640:672, :].astype(F32)
    for k, (ref, at) in enumerate(((late_ref, 0), (early_ref, 0), (early_ref, 640))):
        first_ref[k] = ref[at : at + 384, :].astype(F32)
        rest_ref[k, 0] = ref[at + 384 : at + 512, :].astype(F32)
        rest_ref[k, 1] = ref[at + 512 : at + 640, :].astype(F32)
        bias_ref[k] = small[8 * k : 8 * k + 4, :]
        gain_ref[k : k + 1, :] = small[8 * k + 4 : 8 * k + 5, :]
    for i in range(6, 10):
        given[i].start()
    for came, go in zip(taken[2:], given):
        came.wait()
        go.start()
    for copy in given:
        copy.wait()


VMEM = pl.BlockSpec(memory_space=pltpu.VMEM)
SMEM = pl.BlockSpec(memory_space=pltpu.SMEM)
ANY = pl.BlockSpec(memory_space=pl.ANY)


def shape(rows, dtype):
    return jax.ShapeDtypeStruct((rows, D), dtype)


def per_device(
    node_latents,
    mesh_latents,
    world_latents,
    mesh_src,
    mesh_dst,
    world_src,
    world_dst,
    send_blocks,
    world_count,
    node_cot,
    mesh_cot,
    world_cot,
    first_weights,
    rest_weights,
    biases,
    gains,
):
    n_dom = lax.axis_size("dom")
    n_dp = lax.axis_size("dp")
    n_mesh = mesh_latents.shape[0]
    n_world = world_latents.shape[0]
    steps = n_mesh // ROWS
    half = NODES // 2
    slots = n_dom * CAP
    n_early = n_dp * QUARTER

    def vm(rows, dtype, width=D):
        return pltpu.VMEM((rows, width), dtype)

    def dma(*count):
        return pltpu.SemaphoreType.DMA(count)

    def tiles(count):
        return pltpu.VMEM((count, 8, 128), jnp.int32)

    (
        new_nodes, new_world, grad_nodes, grad_world, early, late, most, new_mesh, grad_mesh
    ) = pl.pallas_call(
        functools.partial(cloth_kernel, n_dom, n_dp),
        out_shape=[
            shape(NODES, BF), shape(n_world, BF), shape(NODES, BF), shape(n_world, BF),
            shape(n_early, BF), shape(N_LATE, BF), jax.ShapeDtypeStruct((1,), jnp.int32),
            shape(n_mesh, BF), shape(n_mesh, BF),
        ],
        in_specs=[SMEM] + [VMEM] * 13 + [ANY] * 2,
        out_specs=[VMEM] * 6 + [SMEM] + [ANY] * 2,
        scratch_shapes=[
            vm(n_mesh, BF), vm(n_mesh, BF), vm(n_mesh, BF), vm(n_mesh, BF),
            vm(n_mesh, BF), vm(n_mesh, BF),
            vm(n_mesh, F32), vm(n_mesh, F32), vm(n_mesh, F32), vm(n_mesh, BF),
            vm(n_mesh, jnp.int32), vm(n_mesh, jnp.int32), vm(slots, jnp.int32),
            vm(n_mesh, BF, half), pltpu.VMEM((steps, half, ROWS), BF),
            vm(half, BF, 2 * D), vm(768, BF, 2 * D),
            vm(half, BF, 2 * D), vm(half, BF, 2 * D),
            vm(slots, BF), vm(slots // 2, BF, 2 * D),
            vm(HALO, BF), vm(HALO, BF),
            pltpu.VMEM((4, 128), jnp.int32), pltpu.VMEM((slots // 128, 128), jnp.int32),
            tiles(n_dom), tiles(n_dom), vm(slots, BF), tiles(n_dp),
            vm(half, F32, 2 * D), vm(768, F32, 2 * D), vm(half, F32, 2 * D),
            vm(640, F32), vm(8, F32),
            vm(slots, BF), vm(slots, BF),
            vm(HALO, BF), vm(HALO, BF), vm(HALO, BF), vm(HALO, BF),
            vm(n_early, BF), vm(n_early, BF), vm(QUARTER, F32), vm(n_dom * EARLY, F32),
            vm(16, F32),
            vm(N_LATE, BF), vm(n_dom * LATE, BF), pltpu.VMEM((n_dp, LATE, D), F32),
            dma(2), dma(2, steps),
            dma(n_dom), dma(n_dom), dma(n_dom), dma(n_dom), dma(2), dma(2), dma(n_dp), dma(n_dp),
            dma(n_dom), dma(n_dom), dma(2), dma(2),
            dma(n_dp), dma(n_dp), dma(n_dom), dma(n_dom), dma(n_dom), dma(n_dom),
            dma(n_dom), dma(n_dom), dma(n_dp), dma(n_dp), dma(n_dom), dma(n_dom),
            dma(n_dp), dma(n_dp),
        ],
        compiler_params=pltpu.CompilerParams(
            collective_id=0, has_side_effects=True, vmem_limit_bytes=58 * 1024 * 1024
        ),
        name="cloth",
    )(
        world_count, world_src.reshape(-1, 128), world_dst.reshape(-1, 128), jnp.transpose(send_blocks[0]),
        mesh_src.reshape(-1, 128), mesh_dst.reshape(-1, 128), node_latents, node_cot,
        world_latents, world_cot, first_weights, rest_weights, biases, gains, mesh_latents,
        mesh_cot,
    )

    def finish():
        arrived = [early, late, new_nodes, new_mesh, new_world, grad_nodes, grad_mesh, grad_world]
        held = [jax.ShapeDtypeStruct(each.shape, each.dtype) for each in arrived]
        weights = [
            jax.ShapeDtypeStruct((3, 3 * D, D), F32),
            jax.ShapeDtypeStruct((3, 2, D, D), F32),
            jax.ShapeDtypeStruct((3, 4, D), F32),
            jax.ShapeDtypeStruct((3, D), F32),
        ]
        return tuple(
            pl.pallas_call(
                finish_kernel,
                out_shape=held[2:] + weights,
                in_specs=[ANY] * 8,
                out_specs=[ANY] * 10,
                scratch_shapes=[pltpu.VMEM(each.shape, each.dtype) for each in held + weights]
                + [dma(8), dma(10)],
                name="finish",
            )(*arrived)
        )

    def start_over():
        return full_exchange(
            node_latents, mesh_latents, world_latents, mesh_src, mesh_dst, world_src, world_dst,
            send_blocks, world_count, node_cot, mesh_cot, world_cot, first_weights, rest_weights,
            biases, gains,
        )

    return lax.cond(most[0] > CAP, start_over, finish)


def solution(mesh):
    part = P(("dom", "dp"))
    rows = P(("dom", "dp"), None)
    return jax.shard_map(
        per_device,
        mesh=mesh,
        in_specs=(
            rows, rows, rows, part, part, part, part, P(("dom", "dp"), None, None), part, rows,
            rows, rows, P(), P(), P(), P(),
        ),
        out_specs=(rows, rows, rows, rows, rows, rows, P(), P(), P(), P()),
        check_vma=False,
    )
```

```python
import functools

import jax
import jax.numpy as jnp
from jax import lax
from jax.experimental import pallas as pl
from jax.experimental.pallas import tpu as pltpu
from jax.sharding import PartitionSpec as P

D = 128
HALO = 256
BLK = 16
ROWS = 512
GROUPS = ROWS // 128
NODES = 1024
CAP = 48
LATE = 32
EARLY = 16
QUARTER = 320
N_LATE = 672
EPS = 1e-05
BF = jnp.bfloat16
F32 = jnp.float32
MESH = pl.DeviceIdType.MESH


def nn(left, right):
    return jnp.dot(left, right, preferred_element_type=F32)


def nt(left, right):
    return lax.dot_general(left, right, (((1,), (1,)), ((), ())), preferred_element_type=F32)


def tn(left, right):
    return lax.dot_general(left, right, (((0,), (0,)), ((), ())), preferred_element_type=F32)


def sigma(values):
    return 0.5 + 0.5 * jnp.tanh(0.5 * values)


def lane_mean(values):
    return jnp.sum(values, axis=-1, keepdims=True) * (1.0 / D)


def columns_of(index_ref, first):
    return [
        jnp.transpose(jnp.broadcast_to(index_ref[pl.ds(first + g, 1), :], (128, 128)))
        for g in range(GROUPS)
    ]


def load_columns(columns_ref, first):
    return [columns_ref[pl.ds(pl.multiple_of(first + g * 128, 128), 128), :] for g in range(GROUPS)]


def fold(index, half):
    return jnp.where(index >= half, index - half, index)


def pick(columns, half):
    lane = lax.broadcasted_iota(jnp.int32, (128, 128), 1).astype(jnp.int16)
    one = jnp.ones((128, 128), BF)
    zero = jnp.zeros((128, 128), BF)
    out = []
    for column in columns:
        low = fold(column, half).astype(jnp.int16)
        out.append(
            jnp.concatenate(
                [jnp.where(low == lane + jnp.int16(b * 128), one, zero) for b in range(half // 128)],
                axis=1,
            )
        )
    return jnp.concatenate(out, axis=0)


def put(index_ref, first, half):
    down = lax.broadcasted_iota(jnp.int32, (128, 128), 0).astype(jnp.int16)
    one = jnp.ones((128, 128), BF)
    zero = jnp.zeros((128, 128), BF)
    out = []
    for g in range(GROUPS):
        row = fold(index_ref[pl.ds(first + g, 1), :], half)
        low = jnp.broadcast_to(row, (128, 128)).astype(jnp.int16)
        out.append(
            jnp.concatenate(
                [jnp.where(low == down + jnp.int16(b * 128), one, zero) for b in range(half // 128)],
                axis=0,
            )
        )
    return jnp.concatenate(out, axis=1)


def gathered(picked, columns, half, table):
    both = nn(picked, table)
    return jnp.concatenate(
        [
            jnp.where(
                column >= half,
                both[g * 128 : (g + 1) * 128, D:],
                both[g * 128 : (g + 1) * 128, :D],
            )
            for g, column in enumerate(columns)
        ],
        axis=0,
    )


def halved(values, columns, half):
    out = []
    for g, column in enumerate(columns):
        rows = values[g * 128 : (g + 1) * 128, :]
        high = column >= half
        out.append(
            jnp.concatenate([jnp.where(high, 0.0, rows), jnp.where(high, rows, 0.0)], axis=1)
        )
    return jnp.concatenate(out, axis=0).astype(BF)


def layers(which, pre_one, rest_ref, bias_ref):
    sig_one = sigma(pre_one)
    act_one = (pre_one * sig_one).astype(BF)
    pre_two = nn(act_one, rest_ref[which, 0]) + bias_ref[which, 1:2, :]
    sig_two = sigma(pre_two)
    act_two = (pre_two * sig_two).astype(BF)
    pre_three = nn(act_two, rest_ref[which, 1]) + bias_ref[which, 2:3, :]
    centred = pre_three - lane_mean(pre_three)
    inv_std = lax.rsqrt(lane_mean(centred * centred) + EPS)
    return sig_one, act_one, pre_two, sig_two, act_two, centred, inv_std


def layers_back(which, cot, pre_one, sig_one, pre_two, sig_two, normed, inv_std, rest_ref, gain_ref):
    scaled = cot * gain_ref[which : which + 1, :]
    d_three = inv_std * (scaled - lane_mean(scaled) - normed * lane_mean(scaled * normed))
    d_three_b = d_three.astype(BF)
    d_two = nt(d_three_b, rest_ref[which, 1]) * (sig_two * (1.0 + pre_two * (1.0 - sig_two)))
    d_two_b = d_two.astype(BF)
    d_one = nt(d_two_b, rest_ref[which, 0]) * (sig_one * (1.0 + pre_one * (1.0 - sig_one)))
    d_one_b = d_one.astype(BF)

    def total(values):
        return jnp.sum(values, axis=0, keepdims=True)

    sums = jnp.concatenate(
        [
            total(d_one),
            total(d_two),
            total(d_three),
            total(cot),
            total(cot * normed),
            jnp.zeros((3, D), F32),
        ],
        axis=0,
    )
    return d_one_b, d_two_b, d_three_b, sums


def span(which, rows):
    return pl.ds(pl.multiple_of(which * rows, rows), rows)


def greet(n_dom, n_dp, dom, dp, barrier):
    @pl.loop(1, n_dom)
    def _(s):
        pl.semaphore_signal(
            barrier, inc=1, device_id=(lax.rem(dom + s, n_dom), dp), device_id_type=MESH
        )

    @pl.loop(1, n_dp)
    def _(s):
        pl.semaphore_signal(
            barrier, inc=1, device_id=(dom, lax.rem(dp + s, n_dp)), device_id_type=MESH
        )


def requests(count_ref, src_ref, slot_ref, ask_ref):
    lane = lax.broadcasted_iota(jnp.int32, (1, 128), 1)
    domain = lax.broadcasted_iota(jnp.int32, (32, 128), 0)
    live_rows = count_ref[0]
    owned, valued = [], []
    for g in range(4):
        row = src_ref[g : g + 1, :]
        live = lane + g * 128 < live_rows
        peer = jnp.where(live, row >> 8, -1)
        hit = jnp.where(jnp.broadcast_to(peer, (32, 128)) == domain, 1.0, 0.0)
        owned.append(hit)
        valued.append(hit * ((row & 255) + 1).astype(F32))
    owned = jnp.concatenate(owned, axis=1)
    valued = jnp.concatenate(valued, axis=1).astype(BF)
    earlier = lax.broadcasted_iota(jnp.int32, (512, 512), 0) < lax.broadcasted_iota(
        jnp.int32, (512, 512), 1
    )
    ahead = nn(owned.astype(BF), jnp.where(earlier, 1.0, 0.0).astype(BF))
    rank = jnp.sum(owned * ahead, axis=0, keepdims=True)
    most = jnp.max(jnp.sum(owned, axis=1, keepdims=True), axis=0, keepdims=True)
    place = lax.broadcasted_iota(jnp.int32, (128, 128), 1)
    placed = []
    for g in range(4):
        row = src_ref[g : g + 1, :]
        order = rank[:, g * 128 : (g + 1) * 128].astype(jnp.int32)
        fits = jnp.logical_and(lane + g * 128 < live_rows, order < CAP)
        slot_ref[g : g + 1, :] = jnp.where(fits, (row >> 8) * CAP + order, -1)
        column = jnp.transpose(jnp.broadcast_to(order, (128, 128)))
        placed.append(jnp.where(column == place, 1.0, 0.0).astype(BF))
    table = nn(valued, jnp.concatenate(placed, axis=0))
    wide = lax.broadcasted_iota(jnp.int32, (32, 128), 1)
    table = jnp.where(wide < CAP, table, 0.0)
    table = jnp.where(wide == 127, jnp.broadcast_to(most, (32, 128)), table).astype(jnp.int32)
    for p in range(32):
        ask_ref[p] = jnp.broadcast_to(table[p : p + 1, :], (8, 128))


def asked_rows(asked_ref, blocks_ref, need_ref):
    table = jnp.concatenate([asked_ref[k, 0:1, :] for k in range(32)], axis=0)
    most = jnp.max(table[:, 127:128], axis=0, keepdims=True)
    wanted = table - 1
    slot = wanted >> 4
    inside = wanted & 15
    eye = lax.broadcasted_iota(jnp.int32, (16, 128), 0) == lax.broadcasted_iota(
        jnp.int32, (16, 128), 1
    )
    blocks = tn(
        blocks_ref[...].astype(F32).astype(BF), jnp.where(eye, 1.0, 0.0).astype(BF)
    ).astype(jnp.int32)
    rows = jnp.full((32, 128), -1, jnp.int32)
    for t in range(16):
        rows = jnp.where(slot == t, blocks[:, t : t + 1] * BLK + inside, rows)
    rolled = {}
    lane = lax.broadcasted_iota(jnp.int32, (1, 128), 1)
    for g in range(32 * CAP // 128):
        line = jnp.full((1, 128), -1, jnp.int32)
        for k in range(32):
            start = k * CAP - g * 128
            if -CAP < start < 128:
                if start % 128 not in rolled:
                    rolled[start % 128] = pltpu.roll(rows, start % 128, 1) if start % 128 else rows
                piece = rolled[start % 128][k : k + 1, :]
                inside_piece = jnp.logical_and(lane >= start, lane < start + CAP)
                line = jnp.where(inside_piece, piece, line)
        need_ref[g : g + 1, :] = line
    return most


def extended(value, sides, width):
    for axis, dim in sides:
        devices, length = (lax.axis_size(axis), value.shape[dim])
        up = [(i, (i + 1) % devices) for i in range(devices - 1)]
        down = [(j, i) for i, j in up]
        last = lax.slice_in_dim(value, length - width, length, axis=dim)
        leading = lax.slice_in_dim(value, 0, width, axis=dim)
        before = lax.ppermute(last, axis, up)
        after = lax.ppermute(leading, axis, down)
        value = jnp.concatenate([before, value, after], axis=dim)
    return value


def from_behind(value, axis, steps):
    count = lax.axis_size(axis)
    leading, last = (max(0, -steps), min(count, count - steps))
    return lax.ppermute(value, axis, [(source, source + steps) for source in range(leading, last)])


def matmul(left, right):
    return jnp.dot(left, right, preferred_element_type=jnp.float32)


def matmul_nt(left, right):
    return lax.dot_general(
        left, right, (((1,), (1,)), ((), ())), preferred_element_type=jnp.float32
    )


def matmul_tn(left, right):
    return lax.dot_general(
        left, right, (((0,), (0,)), ((), ())), preferred_element_type=jnp.float32
    )


def silu_grad(values):
    sigma = jax.nn.sigmoid(values)
    return sigma * (1.0 + values * (1.0 - sigma))


def mlp_parts(inputs, first_w, rest_w, bias_rows, gain_row):
    pre_one = matmul(inputs, first_w) + bias_rows[0]
    act_one = jax.nn.silu(pre_one).astype(jnp.bfloat16)
    pre_two = matmul(act_one, rest_w[0]) + bias_rows[1]
    act_two = jax.nn.silu(pre_two).astype(jnp.bfloat16)
    pre_three = matmul(act_two, rest_w[1]) + bias_rows[2]
    centred = pre_three - jnp.mean(pre_three, axis=-1, keepdims=True)
    inv_std = lax.rsqrt(jnp.mean(centred * centred, axis=-1, keepdims=True) + EPS)
    normed = centred * inv_std
    output = normed * gain_row + bias_rows[3]
    return (output, (pre_one, act_one, pre_two, act_two, normed, inv_std))


def mlp_backward(inputs, first_w, rest_w, bias_rows, gain_row, cotangent):
    _, saved = mlp_parts(inputs, first_w, rest_w, bias_rows, gain_row)
    pre_one, act_one, pre_two, act_two, normed, inv_std = saved
    grad_gain = jnp.sum(cotangent * normed, axis=0)
    grad_shift = jnp.sum(cotangent, axis=0)
    scaled = cotangent * gain_row
    d_three = inv_std * (
        scaled
        - jnp.mean(scaled, axis=-1, keepdims=True)
        - normed * jnp.mean(scaled * normed, axis=-1, keepdims=True)
    )
    d_three_b = d_three.astype(jnp.bfloat16)
    grad_w3 = matmul_tn(act_two, d_three_b)
    d_two = matmul_nt(d_three_b, rest_w[1]) * silu_grad(pre_two)
    d_two_b = d_two.astype(jnp.bfloat16)
    grad_w2 = matmul_tn(act_one, d_two_b)
    d_one = matmul_nt(d_two_b, rest_w[0]) * silu_grad(pre_one)
    d_one_b = d_one.astype(jnp.bfloat16)
    grad_w1 = matmul_tn(inputs, d_one_b)
    grad_in = matmul_nt(d_one_b, first_w)
    bias_grads = jnp.stack(
        [jnp.sum(d_one, axis=0), jnp.sum(d_two, axis=0), jnp.sum(d_three, axis=0), grad_shift]
    )
    return (grad_in, (grad_w1, jnp.stack([grad_w2, grad_w3]), bias_grads, grad_gain))


def full_exchange(
    node_latents,
    mesh_latents,
    world_latents,
    mesh_src,
    mesh_dst,
    world_src,
    world_dst,
    send_blocks,
    world_count,
    node_cot,
    mesh_cot,
    world_cot,
    first_weights,
    rest_weights,
    biases,
    gains,
):
    node_count = node_latents.shape[0]
    latent_width = node_latents.shape[1]
    weights = [
        (first_weights[which], rest_weights[which], biases[which], gains[which])
        for which in range(3)
    ]
    padded = extended(node_latents, (("dom", 0),), HALO)
    send_index = (send_blocks[0][:, :, None] * BLK + jnp.arange(BLK, dtype=jnp.int32)).reshape(-1)
    incoming = lax.all_to_all(
        node_latents[send_index], "dom", split_axis=0, concat_axis=0, tiled=True
    )
    recv_rows = incoming.shape[0]
    mesh_inputs = jnp.concatenate([mesh_latents, padded[mesh_src], node_latents[mesh_dst]], axis=1)
    mesh_message, _ = mlp_parts(mesh_inputs, *weights[0])
    new_mesh = (mesh_latents.astype(jnp.float32) + mesh_message).astype(jnp.bfloat16)
    mesh_total = jax.ops.segment_sum(mesh_message, mesh_dst, num_segments=node_count)
    world_total_rows = world_latents.shape[0]
    live_rows = world_count[0]

    def world_inputs(row_count):
        keep_rows = (jnp.arange(row_count, dtype=jnp.int32) < live_rows).astype(jnp.float32)[
            :, None
        ]
        inputs = jnp.concatenate(
            [world_latents, incoming[world_src], node_latents[world_dst]], axis=1
        )
        return (world_latents, world_src, world_dst, keep_rows, inputs)

    latents, sources, targets, keep_rows, inputs = world_inputs(world_total_rows)
    message = mlp_parts(inputs, *weights[1])[0] * keep_rows
    updated = (latents.astype(jnp.float32) + message).astype(jnp.bfloat16)
    world_total = jax.ops.segment_sum(message, targets, num_segments=node_count)
    node_input = jnp.concatenate(
        [node_latents, mesh_total.astype(jnp.bfloat16), world_total.astype(jnp.bfloat16)], axis=1
    )
    node_update, _ = mlp_parts(node_input, *weights[2])
    new_nodes = (node_latents.astype(jnp.float32) + node_update).astype(jnp.bfloat16)
    node_back, node_grads = mlp_backward(node_input, *weights[2], node_cot.astype(jnp.float32))
    grad_local = node_cot.astype(jnp.float32) + node_back[:, :latent_width]
    mesh_back = node_back[:, latent_width : 2 * latent_width]
    world_back = node_back[:, 2 * latent_width :]
    mesh_upstream = mesh_cot.astype(jnp.float32) + mesh_back[mesh_dst]
    mesh_in_grad, mesh_grads = mlp_backward(mesh_inputs, *weights[0], mesh_upstream)
    grad_mesh = (mesh_cot.astype(jnp.float32) + mesh_in_grad[:, :latent_width]).astype(jnp.bfloat16)
    padded_grad = jax.ops.segment_sum(
        mesh_in_grad[:, latent_width : 2 * latent_width],
        mesh_src,
        num_segments=node_count + 2 * HALO,
    )
    from_right = from_behind(padded_grad[:HALO].astype(jnp.bfloat16), "dom", -1).astype(jnp.float32)
    from_left = from_behind(padded_grad[HALO + node_count :].astype(jnp.bfloat16), "dom", 1).astype(
        jnp.float32
    )
    grad_local = grad_local + padded_grad[HALO : HALO + node_count]
    grad_local = grad_local + jax.ops.segment_sum(
        mesh_in_grad[:, 2 * latent_width :], mesh_dst, num_segments=node_count
    )
    grad_local = grad_local + jnp.pad(from_left, ((0, node_count - HALO), (0, 0)))
    grad_local = grad_local + jnp.pad(from_right, ((node_count - HALO, 0), (0, 0)))
    latents, sources, targets, keep_rows, inputs = world_inputs(world_total_rows)
    cotangent = world_cot.astype(jnp.float32)
    in_grad, weight_grads = mlp_backward(
        inputs, *weights[1], keep_rows * (cotangent + world_back[targets])
    )
    own_grad = (cotangent + in_grad[:, :latent_width]).astype(jnp.bfloat16)
    to_source = jax.ops.segment_sum(
        in_grad[:, latent_width : 2 * latent_width], sources, num_segments=recv_rows
    )
    to_target = jax.ops.segment_sum(
        in_grad[:, 2 * latent_width :], targets, num_segments=node_count
    )
    returned = lax.all_to_all(
        to_source.astype(jnp.bfloat16), "dom", split_axis=0, concat_axis=0, tiled=True
    ).astype(to_source.dtype)
    grad_local = (
        grad_local + to_target + jax.ops.segment_sum(returned, send_index, num_segments=node_count)
    )
    grad_nodes = grad_local.astype(jnp.bfloat16)
    packed = jnp.concatenate(
        [
            jnp.stack([mesh_grads[0], weight_grads[0], node_grads[0]]).reshape(-1, latent_width),
            jnp.stack([mesh_grads[1], weight_grads[1], node_grads[1]]).reshape(-1, latent_width),
            jnp.stack([mesh_grads[2], weight_grads[2], node_grads[2]]).reshape(-1, latent_width),
            jnp.stack([mesh_grads[3], weight_grads[3], node_grads[3]]),
        ]
    )
    devices = lax.axis_size("dom") * lax.axis_size("dp")
    used = packed.shape[0]
    packed = jnp.pad(packed, ((0, -used % (8 * devices)), (0, 0)))
    everyone = ("dom", "dp")
    pieces = lax.all_to_all(packed, everyone, split_axis=0, concat_axis=0, tiled=True)
    piece = jnp.sum(pieces.reshape(devices, -1, latent_width), axis=0) / devices
    total = lax.all_to_all(
        jnp.tile(piece, (devices, 1)), everyone, split_axis=0, concat_axis=0, tiled=True
    )
    first_rows = 9 * latent_width
    rest_rows = first_rows + 6 * latent_width
    return (
        new_nodes,
        new_mesh,
        updated,
        grad_nodes,
        grad_mesh,
        own_grad,
        total[:first_rows].reshape(3, 3 * latent_width, latent_width),
        total[first_rows:rest_rows].reshape(3, 2, latent_width, latent_width),
        total[rest_rows : rest_rows + 12].reshape(3, 4, latent_width),
        total[rest_rows + 12 : used],
    )


def cloth_kernel(
    n_dom, n_dp, count_ref, wsrc_ref, wdst_ref, blocks_ref, src_ref, dst_ref, node_ref,
    node_cot_ref, wlat_ref, wcot_ref, first_ref, rest_ref, bias_ref, gain_ref, lat_hbm, cot_hbm,
    new_nodes_ref, new_world_ref, grad_nodes_ref, grad_world_ref, early_out, late_out, most_ref,
    new_mesh_hbm, grad_mesh_hbm, lat_ref, cot_ref, new_ref, grad_ref, source_ref, target_ref,
    one_ref, two_ref, centred_ref, d_ref, col_src, col_dst, col_need, pick_dst, put_dst, node2,
    ext2, back2, world_back2, got_ref, got2, before_ref, after_ref, slot_ref, need_ref, ask_ref,
    asked_ref, reply_ref, high_ref, acc_dst, acc_src, part2, weight_ref, first_t, sums_ref, sent_ref,
    returned_ref, left_ref, right_ref, from_left_ref, from_right_ref, early, early_got, early_mid,
    early_mid_got, tiny_ref, late, late_got, late_pair, in_s, out_s, ask_s, ask_r, reply_s, reply_r, halo_s, halo_r, high_s,
    high_r, back_s, back_r, rim_s, rim_r, a_s, a_r, b_s, b_r, c_s, c_r, d_s,
    d_r, e_s, e_r, f_s, f_r, g_s, g_r
):
    dom = lax.axis_index("dom")
    dp = lax.axis_index("dp")
    steps = lat_ref.shape[0] // ROWS
    half = NODES // 2
    wide = 768
    slots = CAP * n_dom // 2
    scale = 1.0 / (n_dom * n_dp)
    barrier = pltpu.get_barrier_semaphore()
    greet(n_dom, n_dp, dom, dp, barrier)
    lat_in = pltpu.make_async_copy(lat_hbm, lat_ref, in_s.at[0])
    cot_in = pltpu.make_async_copy(cot_hbm, cot_ref, in_s.at[1])
    lat_in.start()
    cot_in.start()
    requests(count_ref, wsrc_ref, slot_ref, ask_ref)
    pl.semaphore_wait(barrier, n_dom - 1 + n_dp - 1)

    def new_out(c):
        rows = span(c, ROWS)
        return pltpu.make_async_copy(new_ref.at[rows], new_mesh_hbm.at[rows], out_s.at[0, c])

    def grad_out(c):
        rows = span(c, ROWS)
        return pltpu.make_async_copy(grad_ref.at[rows], grad_mesh_hbm.at[rows], out_s.at[1, c])

    def to_domain(from_ref, to_ref, sems, semr, s):
        to = lax.rem(dom + s, n_dom)
        return pltpu.make_async_remote_copy(
            src_ref=from_ref(to), dst_ref=to_ref(dom), send_sem=sems.at[s], recv_sem=semr.at[s],
            device_id=(to, dp), device_id_type=MESH,
        )

    def ask(s):
        return to_domain(lambda to: ask_ref.at[to], lambda me: asked_ref.at[me], ask_s, ask_r, s)

    def reply(s):
        return to_domain(
            lambda to: reply_ref.at[span(to, CAP)], lambda me: got_ref.at[span(me, CAP)],
            reply_s, reply_r, s,
        )

    def give_back(s):
        return to_domain(
            lambda to: sent_ref.at[span(to, CAP)], lambda me: returned_ref.at[span(me, CAP)],
            back_s, back_r, s,
        )

    def scatter(rows, mine, got, sems, semr, s):
        return to_domain(
            lambda to: mine.at[span(lax.rem(to, mine.shape[0] // rows), rows)],
            lambda me: got.at[span(me, rows)], sems, semr, s,
        )

    def spread(rows, out, sems, semr, s):
        at = span(lax.rem(dom, out.shape[0] // rows), rows)
        return to_domain(lambda to: out.at[at], lambda me: out.at[at], sems, semr, s)

    def swap(pair, sems, semr, s):
        return pltpu.make_async_remote_copy(
            src_ref=pair.at[dp], dst_ref=pair.at[dp], send_sem=sems.at[s], recv_sem=semr.at[s],
            device_id=(dom, lax.rem(dp + s, n_dp)), device_id_type=MESH,
        )

    def neighbour(from_ref, to_ref, sems, semr, at, step):
        return pltpu.make_async_remote_copy(
            src_ref=from_ref, dst_ref=to_ref, send_sem=sems.at[at], recv_sem=semr.at[at],
            device_id=(lax.rem(dom + step, n_dom), dp), device_id_type=MESH,
        )

    def collected(rows, mine, got, sems, semr):
        def add(s, total):
            scatter(rows, mine, got, sems, semr, s).wait_recv()
            return total + got[span(lax.rem(dom - s + n_dom, n_dom), rows), :].astype(F32)

        return lax.fori_loop(1, n_dom, add, mine[span(dom, rows), :].astype(F32))

    def quarter(s):
        to = lax.rem(dp + s, n_dp)
        return pltpu.make_async_remote_copy(
            src_ref=early.at[span(to, QUARTER)], dst_ref=early_got.at[span(dp, QUARTER)],
            send_sem=a_s.at[s], recv_sem=a_r.at[s], device_id=(dom, to), device_id_type=MESH,
        )

    def middle(s):
        return scatter(EARLY, early_mid, early_mid_got, b_s, b_r, s)

    def mine():
        return pl.ds(pl.multiple_of(dp * QUARTER + lax.rem(dom, QUARTER // EARLY) * EARLY, EARLY), EARLY)

    def ready(s):
        return to_domain(
            lambda to: early_out.at[mine()], lambda me: early_out.at[mine()], c_s, c_r, s
        )

    def quarters(s):
        rows = span(dp, QUARTER)
        return pltpu.make_async_remote_copy(
            src_ref=early_out.at[rows], dst_ref=early_out.at[rows], send_sem=g_s.at[s],
            recv_sem=g_r.at[s], device_id=(dom, lax.rem(dp + s, n_dp)), device_id_type=MESH,
        )

    def paired(pair, sems, semr):
        for s in range(1, n_dp):
            swap(pair, sems, semr, s).wait_recv()
        total = pair[0]
        for i in range(1, n_dp):
            total = total + pair[i]
        return (total * scale).astype(BF)

    halo_up = neighbour(
        node_ref.at[pl.ds(NODES - HALO, HALO)], before_ref, halo_s, halo_r, 0, 1
    )
    halo_down = neighbour(node_ref.at[pl.ds(0, HALO)], after_ref, halo_s, halo_r, 1, n_dom - 1)


    halo_up.start()
    halo_down.start()

    @pl.loop(1, n_dom)
    def _(s):
        ask(s).start()

    asked_ref[dom] = ask_ref[dom]
    node2[:, :D] = node_ref[:half, :]
    node2[:, D:] = node_ref[half:, :]
    ext2[HALO:, :D] = node_ref[:half, :]
    ext2[:half, D:] = node_ref[half:, :]
    acc_dst[...] = jnp.zeros(acc_dst.shape, F32)

    @pl.loop(0, steps)
    def _(c):
        columns = columns_of(dst_ref, c * GROUPS)
        rows = span(c, ROWS)
        col_dst[rows, :] = jnp.concatenate(columns, axis=0)
        picked = pick(columns, half)
        pick_dst[rows, :] = picked
        target_ref[rows, :] = gathered(picked, columns, half, node2[...]).astype(BF)

    halo_up.wait_recv()
    halo_down.wait_recv()
    ext2[:HALO, :D] = before_ref[...]
    ext2[half:, D:] = after_ref[...]
    lat_in.wait()


    def ahead(c, carry):
        rows = span(c, ROWS)
        columns = columns_of(src_ref, c * GROUPS)
        col_src[rows, :] = jnp.concatenate(columns, axis=0)
        source = gathered(pick(columns, wide), columns, wide, ext2[...]).astype(BF)
        source_ref[rows, :] = source
        lat = lat_ref[rows, :]
        inputs = jnp.concatenate([lat, source, target_ref[rows, :]], axis=1)
        pre_one = nn(inputs, first_ref[0]) + bias_ref[0, 0:1, :]
        _, _, pre_two, _, _, centred, inv_std = layers(0, pre_one, rest_ref, bias_ref)
        message = centred * inv_std * gain_ref[0:1, :] + bias_ref[0, 3:4, :]
        new_ref[rows, :] = (lat.astype(F32) + message).astype(BF)
        new_out(c).start()
        one_ref[rows, :] = pre_one
        two_ref[rows, :] = pre_two
        centred_ref[rows, :] = centred
        spot = put(dst_ref, c * GROUPS, half)
        put_dst[c] = spot
        acc_dst[...] += nn(spot, halved(message, load_columns(col_dst, c * ROWS), half))
        return carry

    lax.fori_loop(0, 1, ahead, 0)

    @pl.loop(1, n_dom)
    def _(s):
        ask(s).wait_recv()

    high_ref[dp] = jnp.broadcast_to(asked_rows(asked_ref, blocks_ref, need_ref), (8, 128))
    for s in range(1, n_dp):
        swap(high_ref, high_s, high_r, s).start()

    @pl.loop(0, need_ref.shape[0] // GROUPS)
    def _(c):
        columns = columns_of(need_ref, c * GROUPS)
        rows = span(c, ROWS)
        col_need[rows, :] = jnp.concatenate(columns, axis=0)
        reply_ref[rows, :] = gathered(pick(columns, half), columns, half, node2[...]).astype(BF)

    @pl.loop(1, n_dom)
    def _(s):
        reply(s).start()

    got_ref[span(dom, CAP), :] = reply_ref[span(dom, CAP), :]
    lax.fori_loop(1, steps, ahead, 0)

    @pl.loop(1, n_dom)
    def _(s):
        reply(s).wait_recv()


    got2[:, :D] = got_ref[:slots, :]
    got2[:, D:] = got_ref[slots:, :]
    live_rows = count_ref[0]
    keep = (lax.broadcasted_iota(jnp.int32, (512, D), 0) < live_rows).astype(F32)
    slot_columns = columns_of(slot_ref, 0)
    world_columns = columns_of(wdst_ref, 0)
    world_pick = pick(world_columns, half)
    world_put = put(wdst_ref, 0, half)
    lat = wlat_ref[...]
    inputs = jnp.concatenate(
        [
            lat,
            gathered(pick(slot_columns, slots), slot_columns, slots, got2[...]).astype(BF),
            gathered(world_pick, world_columns, half, node2[...]).astype(BF),
        ],
        axis=1,
    )
    pre_one = nn(inputs, first_ref[1]) + bias_ref[1, 0:1, :]
    sig_one, act_one, pre_two, sig_two, act_two, centred, inv_std = layers(
        1, pre_one, rest_ref, bias_ref
    )
    normed = centred * inv_std
    message = keep * (normed * gain_ref[1:2, :] + bias_ref[1, 3:4, :])
    new_world_ref[...] = (lat.astype(F32) + message).astype(BF)
    world_sum = nn(world_put, halved(message, world_columns, half)).astype(BF)

    for h in range(2):
        rows = slice(h * half, h * half + half)
        side = slice(h * D, h * D + D)
        node = node_ref[rows, :]
        n_inputs = jnp.concatenate([node, acc_dst[:, side].astype(BF), world_sum[:, side]], axis=1)
        n_one = nn(n_inputs, first_ref[2]) + bias_ref[2, 0:1, :]
        n_sig_one, n_act_one, n_two, n_sig_two, n_act_two, n_centred, n_inv = layers(
            2, n_one, rest_ref, bias_ref
        )
        n_normed = n_centred * n_inv
        new_nodes_ref[rows, :] = (
            node.astype(F32) + n_normed * gain_ref[2:3, :] + bias_ref[2, 3:4, :]
        ).astype(BF)
        n_cot = node_cot_ref[rows, :].astype(F32)
        e_one, e_two, e_three, sums = layers_back(
            2, n_cot, n_one, n_sig_one, n_two, n_sig_two, n_normed, n_inv, rest_ref, gain_ref
        )
        if h == 0:
            weight_ref[: 3 * D, :] = tn(n_inputs, e_one)
            weight_ref[3 * D : 4 * D, :] = tn(n_act_one, e_two)
            weight_ref[4 * D :, :] = tn(n_act_two, e_three)
            sums_ref[...] = sums
        else:
            weight_ref[: 3 * D, :] += tn(n_inputs, e_one)
            weight_ref[3 * D : 4 * D, :] += tn(n_act_one, e_two)
            weight_ref[4 * D :, :] += tn(n_act_two, e_three)
            sums_ref[...] += sums
        part2[:, side] = n_cot + nt(e_one, first_ref[2, :D, :])
        back2[:, side] = nt(e_one, first_ref[2, D : 2 * D, :]).astype(BF)
        world_back2[:, side] = nt(e_one, first_ref[2, 2 * D :, :]).astype(BF)

    own_cot = wcot_ref[...].astype(F32)
    cot = keep * (own_cot + gathered(world_pick, world_columns, half, world_back2[...]))
    d_one, d_two, d_three, sums = layers_back(
        1, cot, pre_one, sig_one, pre_two, sig_two, normed, inv_std, rest_ref, gain_ref
    )
    to_source = nt(d_one, first_ref[1, D : 2 * D, :])
    placed = nn(put(slot_ref, 0, slots), halved(to_source, slot_columns, slots)).astype(BF)
    sent_ref[:slots, :] = placed[:, :D]
    sent_ref[slots:, :] = placed[:, D:]

    early[: 3 * D, :] = tn(inputs, d_one).astype(BF)
    early[3 * D : 4 * D, :] = tn(act_one, d_two).astype(BF)
    early[4 * D : 640, :] = tn(act_two, d_three).astype(BF)
    early[640:1280, :] = weight_ref[...].astype(BF)
    tiny_ref[:8, :] = sums
    tiny_ref[8:, :] = sums_ref[...]
    for s in range(1, n_dp):
        quarter(s).start()

    @pl.loop(1, n_dom)
    def _(s):
        give_back(s).start()

    returned_ref[span(dom, CAP), :] = sent_ref[span(dom, CAP), :]
    grad_world_ref[...] = (own_cot + nt(d_one, first_ref[1, :D, :])).astype(BF)
    to_target = nt(d_one, first_ref[1, 2 * D :, :])
    part2[...] += nn(world_put, halved(to_target, world_columns, half))


    weight_ref[...] = jnp.zeros(weight_ref.shape, F32)
    first_t[...] = jnp.zeros(first_t.shape, F32)
    sums_ref[...] = jnp.zeros(sums_ref.shape, F32)
    acc_dst[...] = jnp.zeros(acc_dst.shape, F32)
    acc_src[...] = jnp.zeros(acc_src.shape, F32)
    cot_in.wait()

    def chunk(c, carry):
        rows = span(c, ROWS)
        own = cot_ref[rows, :].astype(F32)
        columns = load_columns(col_dst, c * ROWS)
        cot = own + gathered(pick_dst[rows, :], columns, half, back2[...])
        pre_one = one_ref[rows, :]
        pre_two = two_ref[rows, :]
        centred = centred_ref[rows, :]
        sig_one = sigma(pre_one)
        sig_two = sigma(pre_two)
        inv_std = lax.rsqrt(lane_mean(centred * centred) + EPS)
        normed = centred * inv_std
        d_one, d_two, d_three, sums = layers_back(
            0, cot, pre_one, sig_one, pre_two, sig_two, normed, inv_std, rest_ref, gain_ref
        )
        d_ref[rows, :] = d_one
        grad_ref[rows, :] = (own + nt(d_one, first_ref[0, :D, :])).astype(BF)
        grad_out(c).start()
        inputs = jnp.concatenate(
            [lat_ref[rows, :], source_ref[rows, :], target_ref[rows, :]], axis=1
        )
        first_t[...] += tn(d_one, inputs)
        weight_ref[3 * D : 4 * D, :] += tn((pre_one * sig_one).astype(BF), d_two)
        weight_ref[4 * D :, :] += tn((pre_two * sig_two).astype(BF), d_three)
        sums_ref[...] += sums
        return carry

    n_early = QUARTER // EARLY
    lax.fori_loop(0, steps // 2, chunk, 0)

    total = early[span(dp, QUARTER), :].astype(F32)
    for s in range(1, n_dp):
        quarter(s).wait_recv()
        total = total + early_got[span(lax.rem(dp - s + n_dp, n_dp), QUARTER), :].astype(F32)
    early_mid[...] = total

    @pl.loop(1, n_dom)
    def _(s):
        @pl.when(lax.rem(dom + s, n_dom) < n_early)
        def _():
            middle(s).start()

    lax.fori_loop(steps // 2, steps, chunk, 0)

    for k in range(3):
        late[k * D : (k + 1) * D, :] = jnp.transpose(first_t[:, k * D : (k + 1) * D]).astype(BF)
    late[3 * D : 640, :] = weight_ref[3 * D :, :].astype(BF)
    late[640:, :] = jnp.concatenate(
        [sums_ref[...], tiny_ref[...], jnp.zeros((N_LATE - 664, D), F32)], axis=0
    ).astype(BF)
    n_late = N_LATE // LATE

    @pl.loop(1, n_dom)
    def _(s):
        @pl.when(lax.rem(dom + s, n_dom) < n_late)
        def _():
            scatter(LATE, late, late_got, d_s, d_r, s).start()

    @pl.when(dom < n_early)
    def _():
        total = collected(EARLY, early_mid, early_mid_got, b_s, b_r)
        early_out[mine(), :] = (total * scale).astype(BF)

        @pl.loop(1, n_dom)
        def _(s):
            ready(s).start()


    @pl.loop(0, steps)
    def _(c):
        columns = load_columns(col_src, c * ROWS)
        values = d_ref[span(c, ROWS), :].astype(F32)
        acc_src[...] += nn(put(src_ref, c * GROUPS, wide), halved(values, columns, wide))

    weight_src = first_ref[0, D : 2 * D, :]
    left_ref[...] = nt(acc_src[:HALO, :D].astype(BF), weight_src).astype(BF)
    right_ref[...] = nt(acc_src[half:, D:].astype(BF), weight_src).astype(BF)
    rim_down = neighbour(left_ref, from_right_ref, rim_s, rim_r, 0, n_dom - 1)
    rim_up = neighbour(right_ref, from_left_ref, rim_s, rim_r, 1, 1)
    rim_down.start()
    rim_up.start()

    @pl.when(dom < n_late)
    def _():
        late_pair[dp] = collected(LATE, late, late_got, d_s, d_r)
        for s in range(1, n_dp):
            swap(late_pair, e_s, e_r, s).start()

    @pl.loop(1, n_dom)
    def _(s):
        @pl.when(lax.rem(dom - s + n_dom, n_dom) < n_early)
        def _():
            ready(s).wait_recv()

    for s in range(1, n_dp):
        quarters(s).start()

    @pl.loop(0, steps)
    def _(c):
        columns = load_columns(col_dst, c * ROWS)
        values = d_ref[span(c, ROWS), :].astype(F32)
        acc_dst[...] += nn(put_dst[c], halved(values, columns, half))

    @pl.when(dom < n_late)
    def _():
        late_out[span(dom, LATE), :] = paired(late_pair, e_s, e_r)

        @pl.loop(1, n_dom)
        def _(s):
            spread(LATE, late_out, f_s, f_r, s).start()

    for h in range(2):
        side = slice(h * D, h * D + D)
        inner = acc_src[HALO:, :D] if h == 0 else acc_src[:half, D:]
        part2[:, side] += nt(inner.astype(BF), weight_src) + nt(
            acc_dst[:, side].astype(BF), first_ref[0, 2 * D :, :]
        )

    @pl.loop(1, n_dom)
    def _(s):
        give_back(s).wait_recv()

    @pl.loop(0, need_ref.shape[0] // GROUPS)
    def _(c):
        columns = load_columns(col_need, c * ROWS)
        values = returned_ref[span(c, ROWS), :].astype(F32)
        part2[...] += nn(put(need_ref, c * GROUPS, half), halved(values, columns, half))

    rim_down.wait()
    rim_up.wait()
    part2[:HALO, :D] += from_left_ref[...].astype(F32)
    part2[half - HALO :, D:] += from_right_ref[...].astype(F32)
    grad_nodes_ref[:half, :] = part2[:, :D].astype(BF)
    grad_nodes_ref[half:, :] = part2[:, D:].astype(BF)

    for s in range(1, n_dp):
        swap(high_ref, high_s, high_r, s).wait()
        quarter(s).wait_send()
        quarters(s).wait()
    high = high_ref[0]
    for i in range(1, n_dp):
        high = jnp.maximum(high, high_ref[i])
    most_ref[0] = jnp.max(high)
    halo_up.wait_send()
    halo_down.wait_send()

    @pl.loop(0, steps)
    def _(c):
        new_out(c).wait()
        grad_out(c).wait()

    @pl.loop(1, n_dom)
    def _(s):
        ask(s).wait_send()
        reply(s).wait_send()
        give_back(s).wait_send()

        @pl.when(lax.rem(dom + s, n_dom) < n_early)
        def _():
            middle(s).wait_send()

        @pl.when(dom < n_early)
        def _():
            ready(s).wait_send()

        @pl.when(lax.rem(dom + s, n_dom) < n_late)
        def _():
            scatter(LATE, late, late_got, d_s, d_r, s).wait_send()

        @pl.when(dom < n_late)
        def _():
            spread(LATE, late_out, f_s, f_r, s).wait_send()

        @pl.when(lax.rem(dom - s + n_dom, n_dom) < n_late)
        def _():
            spread(LATE, late_out, f_s, f_r, s).wait_recv()

    @pl.when(dom < n_late)
    def _():
        for s in range(1, n_dp):
            swap(late_pair, e_s, e_r, s).wait_send()


def finish_kernel(*refs):
    sources, targets, held = refs[:8], refs[8:18], refs[18:30]
    in_s, out_s = refs[30:]
    early_ref, late_ref = held[:2]
    weights = held[8:]
    first_ref, rest_ref, bias_ref, gain_ref = weights
    taken = [pltpu.make_async_copy(sources[i], held[i], in_s.at[i]) for i in range(8)]
    given = [
        pltpu.make_async_copy(from_ref, targets[i], out_s.at[i])
        for i, from_ref in enumerate(list(held[2:8]) + list(weights))
    ]
    for copy in taken:
        copy.start()
    taken[0].wait()
    taken[1].wait()
    small = late_ref[640:672, :].astype(F32)
    for k, (ref, at) in enumerate(((late_ref, 0), (early_ref, 0), (early_ref, 640))):
        first_ref[k] = ref[at : at + 384, :].astype(F32)
        rest_ref[k, 0] = ref[at + 384 : at + 512, :].astype(F32)
        rest_ref[k, 1] = ref[at + 512 : at + 640, :].astype(F32)
        bias_ref[k] = small[8 * k : 8 * k + 4, :]
        gain_ref[k : k + 1, :] = small[8 * k + 4 : 8 * k + 5, :]
    for i in range(6, 10):
        given[i].start()
    for came, go in zip(taken[2:], given):
        came.wait()
        go.start()
    for copy in given:
        copy.wait()


VMEM = pl.BlockSpec(memory_space=pltpu.VMEM)
SMEM = pl.BlockSpec(memory_space=pltpu.SMEM)
ANY = pl.BlockSpec(memory_space=pl.ANY)


def shape(rows, dtype):
    return jax.ShapeDtypeStruct((rows, D), dtype)


def per_device(
    node_latents,
    mesh_latents,
    world_latents,
    mesh_src,
    mesh_dst,
    world_src,
    world_dst,
    send_blocks,
    world_count,
    node_cot,
    mesh_cot,
    world_cot,
    first_weights,
    rest_weights,
    biases,
    gains,
):
    n_dom = lax.axis_size("dom")
    n_dp = lax.axis_size("dp")
    n_mesh = mesh_latents.shape[0]
    n_world = world_latents.shape[0]
    steps = n_mesh // ROWS
    half = NODES // 2
    slots = n_dom * CAP
    n_early = n_dp * QUARTER

    def vm(rows, dtype, width=D):
        return pltpu.VMEM((rows, width), dtype)

    def dma(*count):
        return pltpu.SemaphoreType.DMA(count)

    def tiles(count):
        return pltpu.VMEM((count, 8, 128), jnp.int32)

    (
        new_nodes, new_world, grad_nodes, grad_world, early, late, most, new_mesh, grad_mesh
    ) = pl.pallas_call(
        functools.partial(cloth_kernel, n_dom, n_dp),
        out_shape=[
            shape(NODES, BF), shape(n_world, BF), shape(NODES, BF), shape(n_world, BF),
            shape(n_early, BF), shape(N_LATE, BF), jax.ShapeDtypeStruct((1,), jnp.int32),
            shape(n_mesh, BF), shape(n_mesh, BF),
        ],
        in_specs=[SMEM] + [VMEM] * 13 + [ANY] * 2,
        out_specs=[VMEM] * 6 + [SMEM] + [ANY] * 2,
        scratch_shapes=[
            vm(n_mesh, BF), vm(n_mesh, BF), vm(n_mesh, BF), vm(n_mesh, BF),
            vm(n_mesh, BF), vm(n_mesh, BF),
            vm(n_mesh, F32), vm(n_mesh, F32), vm(n_mesh, F32), vm(n_mesh, BF),
            vm(n_mesh, jnp.int32), vm(n_mesh, jnp.int32), vm(slots, jnp.int32),
            vm(n_mesh, BF, half), pltpu.VMEM((steps, half, ROWS), BF),
            vm(half, BF, 2 * D), vm(768, BF, 2 * D),
            vm(half, BF, 2 * D), vm(half, BF, 2 * D),
            vm(slots, BF), vm(slots // 2, BF, 2 * D),
            vm(HALO, BF), vm(HALO, BF),
            pltpu.VMEM((4, 128), jnp.int32), pltpu.VMEM((slots // 128, 128), jnp.int32),
            tiles(n_dom), tiles(n_dom), vm(slots, BF), tiles(n_dp),
            vm(half, F32, 2 * D), vm(768, F32, 2 * D), vm(half, F32, 2 * D),
            vm(640, F32), vm(D, F32, 3 * D), vm(8, F32),
            vm(slots, BF), vm(slots, BF),
            vm(HALO, BF), vm(HALO, BF), vm(HALO, BF), vm(HALO, BF),
            vm(n_early, BF), vm(n_early, BF), vm(QUARTER, F32), vm(n_dom * EARLY, F32),
            vm(16, F32),
            vm(N_LATE, BF), vm(n_dom * LATE, BF), pltpu.VMEM((n_dp, LATE, D), F32),
            dma(2), dma(2, steps),
            dma(n_dom), dma(n_dom), dma(n_dom), dma(n_dom), dma(2), dma(2), dma(n_dp), dma(n_dp),
            dma(n_dom), dma(n_dom), dma(2), dma(2),
            dma(n_dp), dma(n_dp), dma(n_dom), dma(n_dom), dma(n_dom), dma(n_dom),
            dma(n_dom), dma(n_dom), dma(n_dp), dma(n_dp), dma(n_dom), dma(n_dom),
            dma(n_dp), dma(n_dp),
        ],
        compiler_params=pltpu.CompilerParams(
            collective_id=0, has_side_effects=True, vmem_limit_bytes=58 * 1024 * 1024
        ),
        name="cloth",
    )(
        world_count, world_src.reshape(-1, 128), world_dst.reshape(-1, 128), jnp.transpose(send_blocks[0]),
        mesh_src.reshape(-1, 128), mesh_dst.reshape(-1, 128), node_latents, node_cot,
        world_latents, world_cot, first_weights, rest_weights, biases, gains, mesh_latents,
        mesh_cot,
    )

    def finish():
        arrived = [early, late, new_nodes, new_mesh, new_world, grad_nodes, grad_mesh, grad_world]
        held = [jax.ShapeDtypeStruct(each.shape, each.dtype) for each in arrived]
        weights = [
            jax.ShapeDtypeStruct((3, 3 * D, D), F32),
            jax.ShapeDtypeStruct((3, 2, D, D), F32),
            jax.ShapeDtypeStruct((3, 4, D), F32),
            jax.ShapeDtypeStruct((3, D), F32),
        ]
        return tuple(
            pl.pallas_call(
                finish_kernel,
                out_shape=held[2:] + weights,
                in_specs=[ANY] * 8,
                out_specs=[ANY] * 10,
                scratch_shapes=[pltpu.VMEM(each.shape, each.dtype) for each in held + weights]
                + [dma(8), dma(10)],
                name="finish",
            )(*arrived)
        )

    def start_over():
        return full_exchange(
            node_latents, mesh_latents, world_latents, mesh_src, mesh_dst, world_src, world_dst,
            send_blocks, world_count, node_cot, mesh_cot, world_cot, first_weights, rest_weights,
            biases, gains,
        )

    return lax.cond(most[0] > CAP, start_over, finish)


def solution(mesh):
    part = P(("dom", "dp"))
    rows = P(("dom", "dp"), None)
    return jax.shard_map(
        per_device,
        mesh=mesh,
        in_specs=(
            rows, rows, rows, part, part, part, part, P(("dom", "dp"), None, None), part, rows,
            rows, rows, P(), P(), P(), P(),
        ),
        out_specs=(rows, rows, rows, rows, rows, rows, P(), P(), P(), P()),
        check_vma=False,
    )
```

```python
import functools

import jax
import jax.numpy as jnp
from jax import lax
from jax.experimental import pallas as pl
from jax.experimental.pallas import tpu as pltpu
from jax.sharding import PartitionSpec as P

D = 128
HALO = 256
BLK = 16
ROWS = 512
GROUPS = ROWS // 128
NODES = 1024
CAP = 48
LATE = 32
EARLY = 16
QUARTER = 320
N_LATE = 672
EPS = 1e-05
BF = jnp.bfloat16
F32 = jnp.float32
MESH = pl.DeviceIdType.MESH


def nn(left, right):
    return jnp.dot(left, right, preferred_element_type=F32)


def nt(left, right):
    return lax.dot_general(left, right, (((1,), (1,)), ((), ())), preferred_element_type=F32)


def tn(left, right):
    return lax.dot_general(left, right, (((0,), (0,)), ((), ())), preferred_element_type=F32)


def sigma(values):
    return 0.5 + 0.5 * jnp.tanh(0.5 * values)


def lane_mean(values):
    return jnp.sum(values, axis=-1, keepdims=True) * (1.0 / D)


def columns_of(index_ref, first):
    return [
        jnp.transpose(jnp.broadcast_to(index_ref[pl.ds(first + g, 1), :], (128, 128)))
        for g in range(GROUPS)
    ]


def load_columns(columns_ref, first):
    return [columns_ref[pl.ds(pl.multiple_of(first + g * 128, 128), 128), :] for g in range(GROUPS)]


def fold(index, half):
    return jnp.where(index >= half, index - half, index)


def pick(columns, half):
    lane = lax.broadcasted_iota(jnp.int32, (128, 128), 1).astype(jnp.int16)
    one = jnp.ones((128, 128), BF)
    zero = jnp.zeros((128, 128), BF)
    out = []
    for column in columns:
        low = fold(column, half).astype(jnp.int16)
        out.append(
            jnp.concatenate(
                [jnp.where(low == lane + jnp.int16(b * 128), one, zero) for b in range(half // 128)],
                axis=1,
            )
        )
    return jnp.concatenate(out, axis=0)


def put(index_ref, first, half):
    down = lax.broadcasted_iota(jnp.int32, (128, 128), 0).astype(jnp.int16)
    one = jnp.ones((128, 128), BF)
    zero = jnp.zeros((128, 128), BF)
    out = []
    for g in range(GROUPS):
        row = fold(index_ref[pl.ds(first + g, 1), :], half)
        low = jnp.broadcast_to(row, (128, 128)).astype(jnp.int16)
        out.append(
            jnp.concatenate(
                [jnp.where(low == down + jnp.int16(b * 128), one, zero) for b in range(half // 128)],
                axis=0,
            )
        )
    return jnp.concatenate(out, axis=1)


def gathered(picked, columns, half, table):
    both = nn(picked, table)
    return jnp.concatenate(
        [
            jnp.where(
                column >= half,
                both[g * 128 : (g + 1) * 128, D:],
                both[g * 128 : (g + 1) * 128, :D],
            )
            for g, column in enumerate(columns)
        ],
        axis=0,
    )


def halved(values, columns, half):
    out = []
    for g, column in enumerate(columns):
        rows = values[g * 128 : (g + 1) * 128, :]
        high = column >= half
        out.append(
            jnp.concatenate([jnp.where(high, 0.0, rows), jnp.where(high, rows, 0.0)], axis=1)
        )
    return jnp.concatenate(out, axis=0).astype(BF)


def layers(which, pre_one, rest_ref, bias_ref):
    sig_one = sigma(pre_one)
    act_one = (pre_one * sig_one).astype(BF)
    pre_two = nn(act_one, rest_ref[which, 0]) + bias_ref[which, 1:2, :]
    sig_two = sigma(pre_two)
    act_two = (pre_two * sig_two).astype(BF)
    pre_three = nn(act_two, rest_ref[which, 1]) + bias_ref[which, 2:3, :]
    centred = pre_three - lane_mean(pre_three)
    inv_std = lax.rsqrt(lane_mean(centred * centred) + EPS)
    return sig_one, act_one, pre_two, sig_two, act_two, centred, inv_std


def layers_back(which, cot, pre_one, sig_one, pre_two, sig_two, normed, inv_std, rest_ref, gain_ref):
    scaled = cot * gain_ref[which : which + 1, :]
    d_three = inv_std * (scaled - lane_mean(scaled) - normed * lane_mean(scaled * normed))
    d_three_b = d_three.astype(BF)
    d_two = nt(d_three_b, rest_ref[which, 1]) * (sig_two * (1.0 + pre_two * (1.0 - sig_two)))
    d_two_b = d_two.astype(BF)
    d_one = nt(d_two_b, rest_ref[which, 0]) * (sig_one * (1.0 + pre_one * (1.0 - sig_one)))
    d_one_b = d_one.astype(BF)

    def total(values):
        return jnp.sum(values, axis=0, keepdims=True)

    sums = jnp.concatenate(
        [
            total(d_one),
            total(d_two),
            total(d_three),
            total(cot),
            total(cot * normed),
            jnp.zeros((3, D), F32),
        ],
        axis=0,
    )
    return d_one_b, d_two_b, d_three_b, sums


def span(which, rows):
    return pl.ds(pl.multiple_of(which * rows, rows), rows)


def greet(n_dom, n_dp, dom, dp, barrier):
    @pl.loop(1, n_dom)
    def _(s):
        pl.semaphore_signal(
            barrier, inc=1, device_id=(lax.rem(dom + s, n_dom), dp), device_id_type=MESH
        )

    @pl.loop(1, n_dp)
    def _(s):
        pl.semaphore_signal(
            barrier, inc=1, device_id=(dom, lax.rem(dp + s, n_dp)), device_id_type=MESH
        )


def requests(count_ref, src_ref, slot_ref, ask_ref):
    lane = lax.broadcasted_iota(jnp.int32, (1, 128), 1)
    domain = lax.broadcasted_iota(jnp.int32, (32, 128), 0)
    live_rows = count_ref[0]
    owned, valued = [], []
    for g in range(4):
        row = src_ref[g : g + 1, :]
        live = lane + g * 128 < live_rows
        peer = jnp.where(live, row >> 8, -1)
        hit = jnp.where(jnp.broadcast_to(peer, (32, 128)) == domain, 1.0, 0.0)
        owned.append(hit)
        valued.append(hit * ((row & 255) + 1).astype(F32))
    owned = jnp.concatenate(owned, axis=1)
    valued = jnp.concatenate(valued, axis=1).astype(BF)
    earlier = lax.broadcasted_iota(jnp.int32, (512, 512), 0) < lax.broadcasted_iota(
        jnp.int32, (512, 512), 1
    )
    ahead = nn(owned.astype(BF), jnp.where(earlier, 1.0, 0.0).astype(BF))
    rank = jnp.sum(owned * ahead, axis=0, keepdims=True)
    most = jnp.max(jnp.sum(owned, axis=1, keepdims=True), axis=0, keepdims=True)
    place = lax.broadcasted_iota(jnp.int32, (128, 128), 1)
    placed = []
    for g in range(4):
        row = src_ref[g : g + 1, :]
        order = rank[:, g * 128 : (g + 1) * 128].astype(jnp.int32)
        fits = jnp.logical_and(lane + g * 128 < live_rows, order < CAP)
        slot_ref[g : g + 1, :] = jnp.where(fits, (row >> 8) * CAP + order, -1)
        column = jnp.transpose(jnp.broadcast_to(order, (128, 128)))
        placed.append(jnp.where(column == place, 1.0, 0.0).astype(BF))
    table = nn(valued, jnp.concatenate(placed, axis=0))
    wide = lax.broadcasted_iota(jnp.int32, (32, 128), 1)
    table = jnp.where(wide < CAP, table, 0.0)
    table = jnp.where(wide == 127, jnp.broadcast_to(most, (32, 128)), table).astype(jnp.int32)
    for p in range(32):
        ask_ref[p] = jnp.broadcast_to(table[p : p + 1, :], (8, 128))


def asked_rows(asked_ref, blocks_ref, need_ref):
    table = jnp.concatenate([asked_ref[k, 0:1, :] for k in range(32)], axis=0)
    most = jnp.max(table[:, 127:128], axis=0, keepdims=True)
    wanted = table - 1
    slot = wanted >> 4
    inside = wanted & 15
    eye = lax.broadcasted_iota(jnp.int32, (16, 128), 0) == lax.broadcasted_iota(
        jnp.int32, (16, 128), 1
    )
    blocks = tn(
        blocks_ref[...].astype(F32).astype(BF), jnp.where(eye, 1.0, 0.0).astype(BF)
    ).astype(jnp.int32)
    rows = jnp.full((32, 128), -1, jnp.int32)
    for t in range(16):
        rows = jnp.where(slot == t, blocks[:, t : t + 1] * BLK + inside, rows)
    rolled = {}
    lane = lax.broadcasted_iota(jnp.int32, (1, 128), 1)
    for g in range(32 * CAP // 128):
        line = jnp.full((1, 128), -1, jnp.int32)
        for k in range(32):
            start = k * CAP - g * 128
            if -CAP < start < 128:
                if start % 128 not in rolled:
                    rolled[start % 128] = pltpu.roll(rows, start % 128, 1) if start % 128 else rows
                piece = rolled[start % 128][k : k + 1, :]
                inside_piece = jnp.logical_and(lane >= start, lane < start + CAP)
                line = jnp.where(inside_piece, piece, line)
        need_ref[g : g + 1, :] = line
    return most


def extended(value, sides, width):
    for axis, dim in sides:
        devices, length = (lax.axis_size(axis), value.shape[dim])
        up = [(i, (i + 1) % devices) for i in range(devices - 1)]
        down = [(j, i) for i, j in up]
        last = lax.slice_in_dim(value, length - width, length, axis=dim)
        leading = lax.slice_in_dim(value, 0, width, axis=dim)
        before = lax.ppermute(last, axis, up)
        after = lax.ppermute(leading, axis, down)
        value = jnp.concatenate([before, value, after], axis=dim)
    return value


def from_behind(value, axis, steps):
    count = lax.axis_size(axis)
    leading, last = (max(0, -steps), min(count, count - steps))
    return lax.ppermute(value, axis, [(source, source + steps) for source in range(leading, last)])


def matmul(left, right):
    return jnp.dot(left, right, preferred_element_type=jnp.float32)


def matmul_nt(left, right):
    return lax.dot_general(
        left, right, (((1,), (1,)), ((), ())), preferred_element_type=jnp.float32
    )


def matmul_tn(left, right):
    return lax.dot_general(
        left, right, (((0,), (0,)), ((), ())), preferred_element_type=jnp.float32
    )


def silu_grad(values):
    sigma = jax.nn.sigmoid(values)
    return sigma * (1.0 + values * (1.0 - sigma))


def mlp_parts(inputs, first_w, rest_w, bias_rows, gain_row):
    pre_one = matmul(inputs, first_w) + bias_rows[0]
    act_one = jax.nn.silu(pre_one).astype(jnp.bfloat16)
    pre_two = matmul(act_one, rest_w[0]) + bias_rows[1]
    act_two = jax.nn.silu(pre_two).astype(jnp.bfloat16)
    pre_three = matmul(act_two, rest_w[1]) + bias_rows[2]
    centred = pre_three - jnp.mean(pre_three, axis=-1, keepdims=True)
    inv_std = lax.rsqrt(jnp.mean(centred * centred, axis=-1, keepdims=True) + EPS)
    normed = centred * inv_std
    output = normed * gain_row + bias_rows[3]
    return (output, (pre_one, act_one, pre_two, act_two, normed, inv_std))


def mlp_backward(inputs, first_w, rest_w, bias_rows, gain_row, cotangent):
    _, saved = mlp_parts(inputs, first_w, rest_w, bias_rows, gain_row)
    pre_one, act_one, pre_two, act_two, normed, inv_std = saved
    grad_gain = jnp.sum(cotangent * normed, axis=0)
    grad_shift = jnp.sum(cotangent, axis=0)
    scaled = cotangent * gain_row
    d_three = inv_std * (
        scaled
        - jnp.mean(scaled, axis=-1, keepdims=True)
        - normed * jnp.mean(scaled * normed, axis=-1, keepdims=True)
    )
    d_three_b = d_three.astype(jnp.bfloat16)
    grad_w3 = matmul_tn(act_two, d_three_b)
    d_two = matmul_nt(d_three_b, rest_w[1]) * silu_grad(pre_two)
    d_two_b = d_two.astype(jnp.bfloat16)
    grad_w2 = matmul_tn(act_one, d_two_b)
    d_one = matmul_nt(d_two_b, rest_w[0]) * silu_grad(pre_one)
    d_one_b = d_one.astype(jnp.bfloat16)
    grad_w1 = matmul_tn(inputs, d_one_b)
    grad_in = matmul_nt(d_one_b, first_w)
    bias_grads = jnp.stack(
        [jnp.sum(d_one, axis=0), jnp.sum(d_two, axis=0), jnp.sum(d_three, axis=0), grad_shift]
    )
    return (grad_in, (grad_w1, jnp.stack([grad_w2, grad_w3]), bias_grads, grad_gain))


def full_exchange(
    node_latents,
    mesh_latents,
    world_latents,
    mesh_src,
    mesh_dst,
    world_src,
    world_dst,
    send_blocks,
    world_count,
    node_cot,
    mesh_cot,
    world_cot,
    first_weights,
    rest_weights,
    biases,
    gains,
):
    node_count = node_latents.shape[0]
    latent_width = node_latents.shape[1]
    weights = [
        (first_weights[which], rest_weights[which], biases[which], gains[which])
        for which in range(3)
    ]
    padded = extended(node_latents, (("dom", 0),), HALO)
    send_index = (send_blocks[0][:, :, None] * BLK + jnp.arange(BLK, dtype=jnp.int32)).reshape(-1)
    incoming = lax.all_to_all(
        node_latents[send_index], "dom", split_axis=0, concat_axis=0, tiled=True
    )
    recv_rows = incoming.shape[0]
    mesh_inputs = jnp.concatenate([mesh_latents, padded[mesh_src], node_latents[mesh_dst]], axis=1)
    mesh_message, _ = mlp_parts(mesh_inputs, *weights[0])
    new_mesh = (mesh_latents.astype(jnp.float32) + mesh_message).astype(jnp.bfloat16)
    mesh_total = jax.ops.segment_sum(mesh_message, mesh_dst, num_segments=node_count)
    world_total_rows = world_latents.shape[0]
    live_rows = world_count[0]

    def world_inputs(row_count):
        keep_rows = (jnp.arange(row_count, dtype=jnp.int32) < live_rows).astype(jnp.float32)[
            :, None
        ]
        inputs = jnp.concatenate(
            [world_latents, incoming[world_src], node_latents[world_dst]], axis=1
        )
        return (world_latents, world_src, world_dst, keep_rows, inputs)

    latents, sources, targets, keep_rows, inputs = world_inputs(world_total_rows)
    message = mlp_parts(inputs, *weights[1])[0] * keep_rows
    updated = (latents.astype(jnp.float32) + message).astype(jnp.bfloat16)
    world_total = jax.ops.segment_sum(message, targets, num_segments=node_count)
    node_input = jnp.concatenate(
        [node_latents, mesh_total.astype(jnp.bfloat16), world_total.astype(jnp.bfloat16)], axis=1
    )
    node_update, _ = mlp_parts(node_input, *weights[2])
    new_nodes = (node_latents.astype(jnp.float32) + node_update).astype(jnp.bfloat16)
    node_back, node_grads = mlp_backward(node_input, *weights[2], node_cot.astype(jnp.float32))
    grad_local = node_cot.astype(jnp.float32) + node_back[:, :latent_width]
    mesh_back = node_back[:, latent_width : 2 * latent_width]
    world_back = node_back[:, 2 * latent_width :]
    mesh_upstream = mesh_cot.astype(jnp.float32) + mesh_back[mesh_dst]
    mesh_in_grad, mesh_grads = mlp_backward(mesh_inputs, *weights[0], mesh_upstream)
    grad_mesh = (mesh_cot.astype(jnp.float32) + mesh_in_grad[:, :latent_width]).astype(jnp.bfloat16)
    padded_grad = jax.ops.segment_sum(
        mesh_in_grad[:, latent_width : 2 * latent_width],
        mesh_src,
        num_segments=node_count + 2 * HALO,
    )
    from_right = from_behind(padded_grad[:HALO].astype(jnp.bfloat16), "dom", -1).astype(jnp.float32)
    from_left = from_behind(padded_grad[HALO + node_count :].astype(jnp.bfloat16), "dom", 1).astype(
        jnp.float32
    )
    grad_local = grad_local + padded_grad[HALO : HALO + node_count]
    grad_local = grad_local + jax.ops.segment_sum(
        mesh_in_grad[:, 2 * latent_width :], mesh_dst, num_segments=node_count
    )
    grad_local = grad_local + jnp.pad(from_left, ((0, node_count - HALO), (0, 0)))
    grad_local = grad_local + jnp.pad(from_right, ((node_count - HALO, 0), (0, 0)))
    latents, sources, targets, keep_rows, inputs = world_inputs(world_total_rows)
    cotangent = world_cot.astype(jnp.float32)
    in_grad, weight_grads = mlp_backward(
        inputs, *weights[1], keep_rows * (cotangent + world_back[targets])
    )
    own_grad = (cotangent + in_grad[:, :latent_width]).astype(jnp.bfloat16)
    to_source = jax.ops.segment_sum(
        in_grad[:, latent_width : 2 * latent_width], sources, num_segments=recv_rows
    )
    to_target = jax.ops.segment_sum(
        in_grad[:, 2 * latent_width :], targets, num_segments=node_count
    )
    returned = lax.all_to_all(
        to_source.astype(jnp.bfloat16), "dom", split_axis=0, concat_axis=0, tiled=True
    ).astype(to_source.dtype)
    grad_local = (
        grad_local + to_target + jax.ops.segment_sum(returned, send_index, num_segments=node_count)
    )
    grad_nodes = grad_local.astype(jnp.bfloat16)
    packed = jnp.concatenate(
        [
            jnp.stack([mesh_grads[0], weight_grads[0], node_grads[0]]).reshape(-1, latent_width),
            jnp.stack([mesh_grads[1], weight_grads[1], node_grads[1]]).reshape(-1, latent_width),
            jnp.stack([mesh_grads[2], weight_grads[2], node_grads[2]]).reshape(-1, latent_width),
            jnp.stack([mesh_grads[3], weight_grads[3], node_grads[3]]),
        ]
    )
    devices = lax.axis_size("dom") * lax.axis_size("dp")
    used = packed.shape[0]
    packed = jnp.pad(packed, ((0, -used % (8 * devices)), (0, 0)))
    everyone = ("dom", "dp")
    pieces = lax.all_to_all(packed, everyone, split_axis=0, concat_axis=0, tiled=True)
    piece = jnp.sum(pieces.reshape(devices, -1, latent_width), axis=0) / devices
    total = lax.all_to_all(
        jnp.tile(piece, (devices, 1)), everyone, split_axis=0, concat_axis=0, tiled=True
    )
    first_rows = 9 * latent_width
    rest_rows = first_rows + 6 * latent_width
    return (
        new_nodes,
        new_mesh,
        updated,
        grad_nodes,
        grad_mesh,
        own_grad,
        total[:first_rows].reshape(3, 3 * latent_width, latent_width),
        total[first_rows:rest_rows].reshape(3, 2, latent_width, latent_width),
        total[rest_rows : rest_rows + 12].reshape(3, 4, latent_width),
        total[rest_rows + 12 : used],
    )


def cloth_kernel(
    n_dom, n_dp, count_ref, wsrc_ref, wdst_ref, blocks_ref, src_ref, dst_ref, node_ref,
    node_cot_ref, wlat_ref, wcot_ref, first_ref, rest_ref, bias_ref, gain_ref, lat_hbm, cot_hbm,
    new_nodes_ref, new_world_ref, grad_nodes_ref, grad_world_ref, early_out, late_out, most_ref,
    new_mesh_hbm, grad_mesh_hbm, lat_ref, cot_ref, new_ref, grad_ref, source_ref, target_ref,
    one_ref, two_ref, centred_ref, d_ref, col_src, col_dst, col_need, pick_dst, put_dst, node2,
    ext2, back2, world_back2, got_ref, got2, before_ref, after_ref, slot_ref, need_ref, ask_ref,
    asked_ref, reply_ref, high_ref, acc_dst, acc_src, part2, weight_ref, first_t, sums_ref, sent_ref,
    returned_ref, left_ref, right_ref, from_left_ref, from_right_ref, early, early_got, early_mid,
    early_mid_got, tiny_ref, world_d, late, late_got, late_pair, in_s, out_s, ask_s, ask_r, reply_s, reply_r, halo_s, halo_r, high_s,
    high_r, back_s, back_r, rim_s, rim_r, a_s, a_r, b_s, b_r, c_s, c_r, d_s,
    d_r, e_s, e_r, f_s, f_r, g_s, g_r
):
    dom = lax.axis_index("dom")
    dp = lax.axis_index("dp")
    steps = lat_ref.shape[0] // ROWS
    half = NODES // 2
    wide = 768
    slots = CAP * n_dom // 2
    scale = 1.0 / (n_dom * n_dp)
    barrier = pltpu.get_barrier_semaphore()
    greet(n_dom, n_dp, dom, dp, barrier)
    lat_in = pltpu.make_async_copy(lat_hbm, lat_ref, in_s.at[0])
    cot_in = pltpu.make_async_copy(cot_hbm, cot_ref, in_s.at[1])
    lat_in.start()
    cot_in.start()
    requests(count_ref, wsrc_ref, slot_ref, ask_ref)
    pl.semaphore_wait(barrier, n_dom - 1 + n_dp - 1)

    def new_out(c):
        rows = span(c, ROWS)
        return pltpu.make_async_copy(new_ref.at[rows], new_mesh_hbm.at[rows], out_s.at[0, c])

    def grad_out(c):
        rows = span(c, ROWS)
        return pltpu.make_async_copy(grad_ref.at[rows], grad_mesh_hbm.at[rows], out_s.at[1, c])

    def to_domain(from_ref, to_ref, sems, semr, s):
        to = lax.rem(dom + s, n_dom)
        return pltpu.make_async_remote_copy(
            src_ref=from_ref(to), dst_ref=to_ref(dom), send_sem=sems.at[s], recv_sem=semr.at[s],
            device_id=(to, dp), device_id_type=MESH,
        )

    def ask(s):
        return to_domain(lambda to: ask_ref.at[to], lambda me: asked_ref.at[me], ask_s, ask_r, s)

    def reply(s):
        return to_domain(
            lambda to: reply_ref.at[span(to, CAP)], lambda me: got_ref.at[span(me, CAP)],
            reply_s, reply_r, s,
        )

    def give_back(s):
        return to_domain(
            lambda to: sent_ref.at[span(to, CAP)], lambda me: returned_ref.at[span(me, CAP)],
            back_s, back_r, s,
        )

    def scatter(rows, mine, got, sems, semr, s):
        return to_domain(
            lambda to: mine.at[span(lax.rem(to, mine.shape[0] // rows), rows)],
            lambda me: got.at[span(me, rows)], sems, semr, s,
        )

    def spread(rows, out, sems, semr, s):
        at = span(lax.rem(dom, out.shape[0] // rows), rows)
        return to_domain(lambda to: out.at[at], lambda me: out.at[at], sems, semr, s)

    def swap(pair, sems, semr, s):
        return pltpu.make_async_remote_copy(
            src_ref=pair.at[dp], dst_ref=pair.at[dp], send_sem=sems.at[s], recv_sem=semr.at[s],
            device_id=(dom, lax.rem(dp + s, n_dp)), device_id_type=MESH,
        )

    def neighbour(from_ref, to_ref, sems, semr, at, step):
        return pltpu.make_async_remote_copy(
            src_ref=from_ref, dst_ref=to_ref, send_sem=sems.at[at], recv_sem=semr.at[at],
            device_id=(lax.rem(dom + step, n_dom), dp), device_id_type=MESH,
        )

    def collected(rows, mine, got, sems, semr):
        def add(s, total):
            scatter(rows, mine, got, sems, semr, s).wait_recv()
            return total + got[span(lax.rem(dom - s + n_dom, n_dom), rows), :].astype(F32)

        return lax.fori_loop(1, n_dom, add, mine[span(dom, rows), :].astype(F32))

    def quarter(s):
        to = lax.rem(dp + s, n_dp)
        return pltpu.make_async_remote_copy(
            src_ref=early.at[span(to, QUARTER)], dst_ref=early_got.at[span(dp, QUARTER)],
            send_sem=a_s.at[s], recv_sem=a_r.at[s], device_id=(dom, to), device_id_type=MESH,
        )

    def middle(s):
        return scatter(EARLY, early_mid, early_mid_got, b_s, b_r, s)

    def mine():
        return pl.ds(pl.multiple_of(dp * QUARTER + lax.rem(dom, QUARTER // EARLY) * EARLY, EARLY), EARLY)

    def ready(s):
        return to_domain(
            lambda to: early_out.at[mine()], lambda me: early_out.at[mine()], c_s, c_r, s
        )

    def quarters(s):
        rows = span(dp, QUARTER)
        return pltpu.make_async_remote_copy(
            src_ref=early_out.at[rows], dst_ref=early_out.at[rows], send_sem=g_s.at[s],
            recv_sem=g_r.at[s], device_id=(dom, lax.rem(dp + s, n_dp)), device_id_type=MESH,
        )

    def paired(pair, sems, semr):
        for s in range(1, n_dp):
            swap(pair, sems, semr, s).wait_recv()
        total = pair[0]
        for i in range(1, n_dp):
            total = total + pair[i]
        return (total * scale).astype(BF)

    halo_up = neighbour(
        node_ref.at[pl.ds(NODES - HALO, HALO)], before_ref, halo_s, halo_r, 0, 1
    )
    halo_down = neighbour(node_ref.at[pl.ds(0, HALO)], after_ref, halo_s, halo_r, 1, n_dom - 1)


    halo_up.start()
    halo_down.start()

    @pl.loop(1, n_dom)
    def _(s):
        ask(s).start()

    asked_ref[dom] = ask_ref[dom]
    node2[:, :D] = node_ref[:half, :]
    node2[:, D:] = node_ref[half:, :]
    ext2[HALO:, :D] = node_ref[:half, :]
    ext2[:half, D:] = node_ref[half:, :]
    acc_dst[...] = jnp.zeros(acc_dst.shape, F32)

    @pl.loop(0, steps, unroll=True)
    def _(c):
        columns = columns_of(dst_ref, c * GROUPS)
        rows = span(c, ROWS)
        col_dst[rows, :] = jnp.concatenate(columns, axis=0)
        picked = pick(columns, half)
        pick_dst[rows, :] = picked
        target_ref[rows, :] = gathered(picked, columns, half, node2[...]).astype(BF)

    halo_up.wait_recv()
    halo_down.wait_recv()
    ext2[:HALO, :D] = before_ref[...]
    ext2[half:, D:] = after_ref[...]
    lat_in.wait()


    def ahead(c, carry):
        rows = span(c, ROWS)
        columns = columns_of(src_ref, c * GROUPS)
        col_src[rows, :] = jnp.concatenate(columns, axis=0)
        source = gathered(pick(columns, wide), columns, wide, ext2[...]).astype(BF)
        source_ref[rows, :] = source
        lat = lat_ref[rows, :]
        inputs = jnp.concatenate([lat, source, target_ref[rows, :]], axis=1)
        pre_one = nn(inputs, first_ref[0]) + bias_ref[0, 0:1, :]
        _, _, pre_two, _, _, centred, inv_std = layers(0, pre_one, rest_ref, bias_ref)
        message = centred * inv_std * gain_ref[0:1, :] + bias_ref[0, 3:4, :]
        new_ref[rows, :] = (lat.astype(F32) + message).astype(BF)
        new_out(c).start()
        one_ref[rows, :] = pre_one
        two_ref[rows, :] = pre_two
        centred_ref[rows, :] = centred
        spot = put(dst_ref, c * GROUPS, half)
        put_dst[c] = spot
        acc_dst[...] += nn(spot, halved(message, load_columns(col_dst, c * ROWS), half))
        return carry

    lax.fori_loop(0, 1, ahead, 0)

    @pl.loop(1, n_dom)
    def _(s):
        ask(s).wait_recv()

    high_ref[dp] = jnp.broadcast_to(asked_rows(asked_ref, blocks_ref, need_ref), (8, 128))
    for s in range(1, n_dp):
        swap(high_ref, high_s, high_r, s).start()

    @pl.loop(0, need_ref.shape[0] // GROUPS, unroll=True)
    def _(c):
        columns = columns_of(need_ref, c * GROUPS)
        rows = span(c, ROWS)
        col_need[rows, :] = jnp.concatenate(columns, axis=0)
        reply_ref[rows, :] = gathered(pick(columns, half), columns, half, node2[...]).astype(BF)

    @pl.loop(1, n_dom)
    def _(s):
        reply(s).start()

    got_ref[span(dom, CAP), :] = reply_ref[span(dom, CAP), :]
    lax.fori_loop(1, steps, ahead, 0, unroll=True)

    @pl.loop(1, n_dom)
    def _(s):
        reply(s).wait_recv()


    got2[:, :D] = got_ref[:slots, :]
    got2[:, D:] = got_ref[slots:, :]
    live_rows = count_ref[0]
    keep = (lax.broadcasted_iota(jnp.int32, (512, D), 0) < live_rows).astype(F32)
    slot_columns = columns_of(slot_ref, 0)
    world_columns = columns_of(wdst_ref, 0)
    world_pick = pick(world_columns, half)
    world_put = put(wdst_ref, 0, half)
    lat = wlat_ref[...]
    inputs = jnp.concatenate(
        [
            lat,
            gathered(pick(slot_columns, slots), slot_columns, slots, got2[...]).astype(BF),
            gathered(world_pick, world_columns, half, node2[...]).astype(BF),
        ],
        axis=1,
    )
    pre_one = nn(inputs, first_ref[1]) + bias_ref[1, 0:1, :]
    sig_one, act_one, pre_two, sig_two, act_two, centred, inv_std = layers(
        1, pre_one, rest_ref, bias_ref
    )
    normed = centred * inv_std
    message = keep * (normed * gain_ref[1:2, :] + bias_ref[1, 3:4, :])
    new_world_ref[...] = (lat.astype(F32) + message).astype(BF)
    world_sum = nn(world_put, halved(message, world_columns, half)).astype(BF)

    for h in range(2):
        rows = slice(h * half, h * half + half)
        side = slice(h * D, h * D + D)
        node = node_ref[rows, :]
        n_inputs = jnp.concatenate([node, acc_dst[:, side].astype(BF), world_sum[:, side]], axis=1)
        n_one = nn(n_inputs, first_ref[2]) + bias_ref[2, 0:1, :]
        n_sig_one, n_act_one, n_two, n_sig_two, n_act_two, n_centred, n_inv = layers(
            2, n_one, rest_ref, bias_ref
        )
        n_normed = n_centred * n_inv
        new_nodes_ref[rows, :] = (
            node.astype(F32) + n_normed * gain_ref[2:3, :] + bias_ref[2, 3:4, :]
        ).astype(BF)
        n_cot = node_cot_ref[rows, :].astype(F32)
        e_one, e_two, e_three, sums = layers_back(
            2, n_cot, n_one, n_sig_one, n_two, n_sig_two, n_normed, n_inv, rest_ref, gain_ref
        )
        if h == 0:
            weight_ref[: 3 * D, :] = tn(n_inputs, e_one)
            weight_ref[3 * D : 4 * D, :] = tn(n_act_one, e_two)
            weight_ref[4 * D :, :] = tn(n_act_two, e_three)
            sums_ref[...] = sums
        else:
            weight_ref[: 3 * D, :] += tn(n_inputs, e_one)
            weight_ref[3 * D : 4 * D, :] += tn(n_act_one, e_two)
            weight_ref[4 * D :, :] += tn(n_act_two, e_three)
            sums_ref[...] += sums
        part2[:, side] = n_cot + nt(e_one, first_ref[2, :D, :])
        back2[:, side] = nt(e_one, first_ref[2, D : 2 * D, :]).astype(BF)
        world_back2[:, side] = nt(e_one, first_ref[2, 2 * D :, :]).astype(BF)

    early[640:1280, :] = weight_ref[...].astype(BF)
    for s in range(1, n_dp):

        @pl.when(lax.rem(dp + s, n_dp) >= n_dp // 2)
        def _():
            quarter(s).start()

    own_cot = wcot_ref[...].astype(F32)
    cot = keep * (own_cot + gathered(world_pick, world_columns, half, world_back2[...]))
    d_one, d_two, d_three, sums = layers_back(
        1, cot, pre_one, sig_one, pre_two, sig_two, normed, inv_std, rest_ref, gain_ref
    )
    to_source = nt(d_one, first_ref[1, D : 2 * D, :])
    placed = nn(put(slot_ref, 0, slots), halved(to_source, slot_columns, slots)).astype(BF)
    sent_ref[:slots, :] = placed[:, :D]
    sent_ref[slots:, :] = placed[:, D:]

    early[: 3 * D, :] = tn(inputs, d_one).astype(BF)
    early[3 * D : 4 * D, :] = tn(act_one, d_two).astype(BF)
    early[4 * D : 640, :] = tn(act_two, d_three).astype(BF)
    tiny_ref[:8, :] = sums
    tiny_ref[8:, :] = sums_ref[...]
    for s in range(1, n_dp):

        @pl.when(lax.rem(dp + s, n_dp) < n_dp // 2)
        def _():
            quarter(s).start()

    @pl.loop(1, n_dom)
    def _(s):
        give_back(s).start()

    returned_ref[span(dom, CAP), :] = sent_ref[span(dom, CAP), :]
    world_d[...] = d_one


    weight_ref[...] = jnp.zeros(weight_ref.shape, F32)
    first_t[...] = jnp.zeros(first_t.shape, F32)
    sums_ref[...] = jnp.zeros(sums_ref.shape, F32)
    acc_dst[...] = jnp.zeros(acc_dst.shape, F32)
    acc_src[...] = jnp.zeros(acc_src.shape, F32)
    cot_in.wait()

    def chunk(c, carry):
        rows = span(c, ROWS)
        own = cot_ref[rows, :].astype(F32)
        columns = load_columns(col_dst, c * ROWS)
        cot = own + gathered(pick_dst[rows, :], columns, half, back2[...])
        pre_one = one_ref[rows, :]
        pre_two = two_ref[rows, :]
        centred = centred_ref[rows, :]
        sig_one = sigma(pre_one)
        sig_two = sigma(pre_two)
        inv_std = lax.rsqrt(lane_mean(centred * centred) + EPS)
        normed = centred * inv_std
        d_one, d_two, d_three, sums = layers_back(
            0, cot, pre_one, sig_one, pre_two, sig_two, normed, inv_std, rest_ref, gain_ref
        )
        d_ref[rows, :] = d_one
        inputs = jnp.concatenate(
            [lat_ref[rows, :], source_ref[rows, :], target_ref[rows, :]], axis=1
        )
        first_t[...] += tn(d_one, inputs)
        weight_ref[3 * D : 4 * D, :] += tn((pre_one * sig_one).astype(BF), d_two)
        weight_ref[4 * D :, :] += tn((pre_two * sig_two).astype(BF), d_three)
        sums_ref[...] += sums
        return carry

    n_early = QUARTER // EARLY
    lax.fori_loop(0, 2 * steps // 3, chunk, 0, unroll=True)

    total = early[span(dp, QUARTER), :].astype(F32)
    for s in range(1, n_dp):
        quarter(s).wait_recv()
        total = total + early_got[span(lax.rem(dp - s + n_dp, n_dp), QUARTER), :].astype(F32)
    early_mid[...] = total

    @pl.loop(1, n_dom)
    def _(s):
        @pl.when(lax.rem(dom + s, n_dom) < n_early)
        def _():
            middle(s).start()

    lax.fori_loop(2 * steps // 3, steps, chunk, 0, unroll=True)

    for k in range(3):
        late[k * D : (k + 1) * D, :] = jnp.transpose(first_t[:, k * D : (k + 1) * D]).astype(BF)
    late[3 * D : 640, :] = weight_ref[3 * D :, :].astype(BF)
    late[640:, :] = jnp.concatenate(
        [sums_ref[...], tiny_ref[...], jnp.zeros((N_LATE - 664, D), F32)], axis=0
    ).astype(BF)
    n_late = N_LATE // LATE

    @pl.loop(1, n_dom)
    def _(s):
        @pl.when(lax.rem(dom + s, n_dom) < n_late)
        def _():
            scatter(LATE, late, late_got, d_s, d_r, s).start()


    @pl.loop(0, steps, unroll=True)
    def _(c):
        rows = span(c, ROWS)
        columns = load_columns(col_src, c * ROWS)
        d_one = d_ref[rows, :]
        values = d_one.astype(F32)
        own = cot_ref[rows, :].astype(F32)
        grad_ref[rows, :] = (own + nt(d_one, first_ref[0, :D, :])).astype(BF)
        grad_out(c).start()
        acc_src[...] += nn(put(src_ref, c * GROUPS, wide), halved(values, columns, wide))

    weight_src = first_ref[0, D : 2 * D, :]
    left_ref[...] = nt(acc_src[:HALO, :D].astype(BF), weight_src).astype(BF)
    right_ref[...] = nt(acc_src[half:, D:].astype(BF), weight_src).astype(BF)
    rim_down = neighbour(left_ref, from_right_ref, rim_s, rim_r, 0, n_dom - 1)
    rim_up = neighbour(right_ref, from_left_ref, rim_s, rim_r, 1, 1)
    rim_down.start()
    rim_up.start()

    @pl.when(dom < n_early)
    def _():
        total = collected(EARLY, early_mid, early_mid_got, b_s, b_r)
        early_out[mine(), :] = (total * scale).astype(BF)

        @pl.loop(1, n_dom)
        def _(s):
            ready(s).start()

    @pl.when(dom < n_late)
    def _():
        late_pair[dp] = collected(LATE, late, late_got, d_s, d_r)
        for s in range(1, n_dp):
            swap(late_pair, e_s, e_r, s).start()

    @pl.loop(0, steps, unroll=True)
    def _(c):
        columns = load_columns(col_dst, c * ROWS)
        values = d_ref[span(c, ROWS), :].astype(F32)
        acc_dst[...] += nn(put_dst[c], halved(values, columns, half))

    @pl.loop(1, n_dom)
    def _(s):
        @pl.when(lax.rem(dom - s + n_dom, n_dom) < n_early)
        def _():
            ready(s).wait_recv()

    for s in range(1, n_dp):
        quarters(s).start()

    @pl.when(dom < n_late)
    def _():
        late_out[span(dom, LATE), :] = paired(late_pair, e_s, e_r)

        @pl.loop(1, n_dom)
        def _(s):
            spread(LATE, late_out, f_s, f_r, s).start()

    d_world = world_d[...]
    grad_world_ref[...] = (
        wcot_ref[...].astype(F32) + nt(d_world, first_ref[1, :D, :])
    ).astype(BF)
    to_target = nt(d_world, first_ref[1, 2 * D :, :])
    columns = columns_of(wdst_ref, 0)
    part2[...] += nn(put(wdst_ref, 0, half), halved(to_target, columns, half))

    for h in range(2):
        side = slice(h * D, h * D + D)
        inner = acc_src[HALO:, :D] if h == 0 else acc_src[:half, D:]
        part2[:, side] += nt(inner.astype(BF), weight_src) + nt(
            acc_dst[:, side].astype(BF), first_ref[0, 2 * D :, :]
        )

    @pl.loop(1, n_dom)
    def _(s):
        give_back(s).wait_recv()

    @pl.loop(0, need_ref.shape[0] // GROUPS, unroll=True)
    def _(c):
        columns = load_columns(col_need, c * ROWS)
        values = returned_ref[span(c, ROWS), :].astype(F32)
        part2[...] += nn(put(need_ref, c * GROUPS, half), halved(values, columns, half))

    rim_down.wait()
    rim_up.wait()
    part2[:HALO, :D] += from_left_ref[...].astype(F32)
    part2[half - HALO :, D:] += from_right_ref[...].astype(F32)
    grad_nodes_ref[:half, :] = part2[:, :D].astype(BF)
    grad_nodes_ref[half:, :] = part2[:, D:].astype(BF)

    for s in range(1, n_dp):
        swap(high_ref, high_s, high_r, s).wait()
        quarter(s).wait_send()
        quarters(s).wait()
    high = high_ref[0]
    for i in range(1, n_dp):
        high = jnp.maximum(high, high_ref[i])
    most_ref[0] = jnp.max(high)
    halo_up.wait_send()
    halo_down.wait_send()

    @pl.loop(0, steps, unroll=True)
    def _(c):
        new_out(c).wait()
        grad_out(c).wait()

    @pl.loop(1, n_dom)
    def _(s):
        ask(s).wait_send()
        reply(s).wait_send()
        give_back(s).wait_send()

        @pl.when(lax.rem(dom + s, n_dom) < n_early)
        def _():
            middle(s).wait_send()

        @pl.when(dom < n_early)
        def _():
            ready(s).wait_send()

        @pl.when(lax.rem(dom + s, n_dom) < n_late)
        def _():
            scatter(LATE, late, late_got, d_s, d_r, s).wait_send()

        @pl.when(dom < n_late)
        def _():
            spread(LATE, late_out, f_s, f_r, s).wait_send()

        @pl.when(lax.rem(dom - s + n_dom, n_dom) < n_late)
        def _():
            spread(LATE, late_out, f_s, f_r, s).wait_recv()

    @pl.when(dom < n_late)
    def _():
        for s in range(1, n_dp):
            swap(late_pair, e_s, e_r, s).wait_send()


def finish_kernel(*refs):
    sources, targets, held = refs[:8], refs[8:18], refs[18:30]
    in_s, out_s = refs[30:]
    early_ref, late_ref = held[:2]
    weights = held[8:]
    first_ref, rest_ref, bias_ref, gain_ref = weights
    taken = [pltpu.make_async_copy(sources[i], held[i], in_s.at[i]) for i in range(8)]
    given = [
        pltpu.make_async_copy(from_ref, targets[i], out_s.at[i])
        for i, from_ref in enumerate(list(held[2:8]) + list(weights))
    ]
    for copy in taken:
        copy.start()
    taken[0].wait()
    taken[1].wait()
    small = late_ref[640:672, :].astype(F32)
    for k, (ref, at) in enumerate(((late_ref, 0), (early_ref, 0), (early_ref, 640))):
        first_ref[k] = ref[at : at + 384, :].astype(F32)
        rest_ref[k, 0] = ref[at + 384 : at + 512, :].astype(F32)
        rest_ref[k, 1] = ref[at + 512 : at + 640, :].astype(F32)
        bias_ref[k] = small[8 * k : 8 * k + 4, :]
        gain_ref[k : k + 1, :] = small[8 * k + 4 : 8 * k + 5, :]
    for i in range(6, 10):
        given[i].start()
    for came, go in zip(taken[2:], given):
        came.wait()
        go.start()
    for copy in given:
        copy.wait()


VMEM = pl.BlockSpec(memory_space=pltpu.VMEM)
SMEM = pl.BlockSpec(memory_space=pltpu.SMEM)
ANY = pl.BlockSpec(memory_space=pl.ANY)


def shape(rows, dtype):
    return jax.ShapeDtypeStruct((rows, D), dtype)


def per_device(
    node_latents,
    mesh_latents,
    world_latents,
    mesh_src,
    mesh_dst,
    world_src,
    world_dst,
    send_blocks,
    world_count,
    node_cot,
    mesh_cot,
    world_cot,
    first_weights,
    rest_weights,
    biases,
    gains,
):
    n_dom = lax.axis_size("dom")
    n_dp = lax.axis_size("dp")
    n_mesh = mesh_latents.shape[0]
    n_world = world_latents.shape[0]
    steps = n_mesh // ROWS
    half = NODES // 2
    slots = n_dom * CAP
    n_early = n_dp * QUARTER

    def vm(rows, dtype, width=D):
        return pltpu.VMEM((rows, width), dtype)

    def dma(*count):
        return pltpu.SemaphoreType.DMA(count)

    def tiles(count):
        return pltpu.VMEM((count, 8, 128), jnp.int32)

    (
        new_nodes, new_world, grad_nodes, grad_world, early, late, most, new_mesh, grad_mesh
    ) = pl.pallas_call(
        functools.partial(cloth_kernel, n_dom, n_dp),
        out_shape=[
            shape(NODES, BF), shape(n_world, BF), shape(NODES, BF), shape(n_world, BF),
            shape(n_early, BF), shape(N_LATE, BF), jax.ShapeDtypeStruct((1,), jnp.int32),
            shape(n_mesh, BF), shape(n_mesh, BF),
        ],
        in_specs=[SMEM] + [VMEM] * 13 + [ANY] * 2,
        out_specs=[VMEM] * 6 + [SMEM] + [ANY] * 2,
        scratch_shapes=[
            vm(n_mesh, BF), vm(n_mesh, BF), vm(n_mesh, BF), vm(n_mesh, BF),
            vm(n_mesh, BF), vm(n_mesh, BF),
            vm(n_mesh, F32), vm(n_mesh, F32), vm(n_mesh, F32), vm(n_mesh, BF),
            vm(n_mesh, jnp.int32), vm(n_mesh, jnp.int32), vm(slots, jnp.int32),
            vm(n_mesh, BF, half), pltpu.VMEM((steps, half, ROWS), BF),
            vm(half, BF, 2 * D), vm(768, BF, 2 * D),
            vm(half, BF, 2 * D), vm(half, BF, 2 * D),
            vm(slots, BF), vm(slots // 2, BF, 2 * D),
            vm(HALO, BF), vm(HALO, BF),
            pltpu.VMEM((4, 128), jnp.int32), pltpu.VMEM((slots // 128, 128), jnp.int32),
            tiles(n_dom), tiles(n_dom), vm(slots, BF), tiles(n_dp),
            vm(half, F32, 2 * D), vm(768, F32, 2 * D), vm(half, F32, 2 * D),
            vm(640, F32), vm(D, F32, 3 * D), vm(8, F32),
            vm(slots, BF), vm(slots, BF),
            vm(HALO, BF), vm(HALO, BF), vm(HALO, BF), vm(HALO, BF),
            vm(n_early, BF), vm(n_early, BF), vm(QUARTER, F32), vm(n_dom * EARLY, F32),
            vm(16, F32), vm(n_world, BF),
            vm(N_LATE, BF), vm(n_dom * LATE, BF), pltpu.VMEM((n_dp, LATE, D), F32),
            dma(2), dma(2, steps),
            dma(n_dom), dma(n_dom), dma(n_dom), dma(n_dom), dma(2), dma(2), dma(n_dp), dma(n_dp),
            dma(n_dom), dma(n_dom), dma(2), dma(2),
            dma(n_dp), dma(n_dp), dma(n_dom), dma(n_dom), dma(n_dom), dma(n_dom),
            dma(n_dom), dma(n_dom), dma(n_dp), dma(n_dp), dma(n_dom), dma(n_dom),
            dma(n_dp), dma(n_dp),
        ],
        compiler_params=pltpu.CompilerParams(
            collective_id=0, has_side_effects=True, vmem_limit_bytes=58 * 1024 * 1024
        ),
        name="cloth",
    )(
        world_count, world_src.reshape(-1, 128), world_dst.reshape(-1, 128), jnp.transpose(send_blocks[0]),
        mesh_src.reshape(-1, 128), mesh_dst.reshape(-1, 128), node_latents, node_cot,
        world_latents, world_cot, first_weights, rest_weights, biases, gains, mesh_latents,
        mesh_cot,
    )

    def finish():
        arrived = [early, late, new_nodes, new_mesh, new_world, grad_nodes, grad_mesh, grad_world]
        held = [jax.ShapeDtypeStruct(each.shape, each.dtype) for each in arrived]
        weights = [
            jax.ShapeDtypeStruct((3, 3 * D, D), F32),
            jax.ShapeDtypeStruct((3, 2, D, D), F32),
            jax.ShapeDtypeStruct((3, 4, D), F32),
            jax.ShapeDtypeStruct((3, D), F32),
        ]
        return tuple(
            pl.pallas_call(
                finish_kernel,
                out_shape=held[2:] + weights,
                in_specs=[ANY] * 8,
                out_specs=[ANY] * 10,
                scratch_shapes=[pltpu.VMEM(each.shape, each.dtype) for each in held + weights]
                + [dma(8), dma(10)],
                name="finish",
            )(*arrived)
        )

    def start_over():
        return full_exchange(
            node_latents, mesh_latents, world_latents, mesh_src, mesh_dst, world_src, world_dst,
            send_blocks, world_count, node_cot, mesh_cot, world_cot, first_weights, rest_weights,
            biases, gains,
        )

    return lax.cond(most[0] > CAP, start_over, finish)


def solution(mesh):
    part = P(("dom", "dp"))
    rows = P(("dom", "dp"), None)
    return jax.shard_map(
        per_device,
        mesh=mesh,
        in_specs=(
            rows, rows, rows, part, part, part, part, P(("dom", "dp"), None, None), part, rows,
            rows, rows, P(), P(), P(), P(),
        ),
        out_specs=(rows, rows, rows, rows, rows, rows, P(), P(), P(), P()),
        check_vma=False,
    )
```
